32 devices in a mesh: train: 16 (over z, y, core), cand: 2 (over x).
Axes of the slice: x: 2, y: 2, z: 4, core: 2. Of those that a mesh axis runs over, the one named last changes fastest.
Arguments:
- x_train: float32 [8, 2048], P(None, 'train'), may hold values from -4 to 4
- x_cand: float32 [8, 1024], P(None, 'cand'), may hold values from -4 to 4
- targets: float32 [2048], P(('train', 'cand')), may hold values from -6 to 6
- noise: float32 [2048, 64], P(('train', 'cand')), may hold values from -5 to 5
- omega: float32 [8, 4096], replicated, may hold values from -6 to 6
- phase: float32 [4096], replicated, may hold values from -3.140625 to 3.140625
- prior_weights: bfloat16 [4096, 64], P('cand'), may hold values from -6 to 6
Outputs:
- samples: float32 [1024, 64], P(('cand', 'train'))
- solution: float32 [2048, 64], P(('train', 'cand'))
The draws below stay inside these ranges and needn't reach their ends.
All inputs are finite; a program needn't handle non-finite values.
Results may differ from the reference program's by a relative error of at most 0.0019.
The reference program's roundings to bfloat16 on the way count: a program that leaves them out, or rounds other values in their place, can miss the bound.
Values may be sent and summed in bfloat16 or wider, within the bound.
No kernel may reach another device: no remote copies, remote signals or barrier semaphores. Data moves between devices by JAX's collectives and lax.ppermute only.
A program may use at most 64 MiB of HBM per device.

```python
import math
import jax
import jax.numpy as jnp
from jax import lax

DIM = 8
S = 64
F = 4096
ITERS = 2
N = 2048
C = 1024


def shard_levels(key, extent, shards, low, largest):
    factor_of, own = 1.0, jax.random.fold_in(key, 6)
    for dim, parts in shards:
        heights = jnp.exp(jax.random.uniform(jax.random.fold_in(own, dim), (parts,), jnp.float32, low / len(shards), largest / len(shards)))
        factor_of = factor_of * jnp.repeat(heights, extent[dim] // parts).reshape([-1 if axis == dim else 1 for axis in range(len(extent))])
    return factor_of


def gaussian(key, dims, spread, limit, pieces=(), held_as=jnp.bfloat16):
    entries = spread * jax.random.normal(key, dims, jnp.float32)
    if pieces:
        entries = entries * shard_levels(key, dims, pieces, -0.22, 0.18)
    return jnp.clip(entries, -limit, limit).astype(held_as)


def setup_inputs(seed: int = 0) -> dict:
    keys = jax.random.split(jax.random.key(seed), 8)
    x_train = gaussian(keys[0], (DIM, N), 0.7, 4.0, ((1, 16),), jnp.float32)
    x_cand = gaussian(keys[1], (DIM, C), 0.7, 4.0, ((1, 2),), jnp.float32)
    targets = gaussian(keys[2], (N,), 1.0, 6.0, ((0, 32),), jnp.float32)
    noise = gaussian(keys[3], (N, S), 0.7, 5.0, ((0, 32),), jnp.float32)
    omega = gaussian(keys[4], (DIM, F), 1.0, 6.0, (), jnp.float32)
    phase = jnp.clip(jax.random.uniform(keys[5], (F,), jnp.float32, -3.140625, 3.140625), -3.140625, 3.140625)
    prior_weights = gaussian(keys[6], (F, S), 1.0, 6.0, ((0, 2),))
    return dict(x_train=x_train, x_cand=x_cand, targets=targets, noise=noise, omega=omega, phase=phase, prior_weights=prior_weights)


noise_level = 0.5

def squares_of(points):
    return lax.optimization_barrier(jnp.sum(points * points, axis=0))

def kernel_tile(row_points, row_norms, column_points, column_norms):
    inner = jnp.dot(row_points.T, column_points, precision=lax.Precision.HIGHEST)
    return jnp.exp(-0.5 * (row_norms[:, None] + column_norms[None, :] - 2.0 * inner)).astype(jnp.bfloat16)

def features(points, omega, phase):
    angles = jnp.dot(points.T, omega, precision=lax.Precision.HIGHEST) + phase[None, :]
    return (math.sqrt(2.0 / omega.shape[1]) * jnp.cos(angles)).astype(jnp.bfloat16)

def split_points(points, size):
    total = points.shape[1]
    return points.reshape(points.shape[0], total // size, size).transpose(1, 0, 2)

def reference(x_train, x_cand, targets, noise, omega, phase, prior_weights):
    train_size = math.gcd(N, 1024)
    train_blocks = split_points(x_train, train_size)
    train_norms = squares_of(x_train)

    def prior_block(points):
        return jnp.dot(features(points, omega, phase), prior_weights, preferred_element_type=jnp.float32)
    prior_train = lax.map(prior_block, train_blocks).reshape(N, S)
    rhs = targets[:, None] - prior_train - noise

    def apply(direction):
        packed = direction.astype(jnp.bfloat16)

        def rows_of(points):
            tile = kernel_tile(points, squares_of(points), x_train, train_norms)
            return jnp.dot(tile, packed, preferred_element_type=jnp.float32)
        return lax.map(rows_of, train_blocks).reshape(N, S) + noise_level * direction
    solution = jnp.zeros((N, S), jnp.float32)
    residual = rhs
    direction = rhs
    norm_now = lax.optimization_barrier(jnp.sum(residual * residual, axis=0))
    for step in range(ITERS):
        image = apply(direction)
        alpha = norm_now / lax.optimization_barrier(jnp.sum(direction * image, axis=0))
        solution = solution + alpha * direction
        residual = residual - alpha * image
        norm_next = lax.optimization_barrier(jnp.sum(residual * residual, axis=0))
        direction = residual + norm_next / norm_now * direction
        norm_now = norm_next
    packed_solution = solution.astype(jnp.bfloat16)
    cand_size = math.gcd(C, 1024)

    def cand_block(points):
        tile = kernel_tile(points, squares_of(points), x_train, train_norms)
        return prior_block(points) + jnp.dot(tile, packed_solution, preferred_element_type=jnp.float32)
    samples = lax.map(cand_block, split_points(x_cand, cand_size)).reshape(C, S)
    return (samples, solution)
```

```python
import functools
import math

import jax
import jax.numpy as jnp
from jax import lax
from jax.experimental import pallas as pl
from jax.experimental.pallas import tpu as pltpu
from jax.sharding import PartitionSpec as P

ITERS = 2


noise_level = 0.5
LOG2E = math.log2(math.e)
COS = (
    1.0,
    -19.739208743087787,
    64.93938905249153,
    -85.45665775372363,
    60.24212493122888,
    -26.404630623401626,
    7.8000222194698186,
    -1.4529875517062139,
)
KERNEL_BYTES = 16 << 20
f32, bf16 = jnp.float32, jnp.bfloat16


def split3(values):
    high = values.astype(bf16)
    rest = values - high.astype(f32)
    middle = rest.astype(bf16)
    low = (rest - middle.astype(f32)).astype(bf16)
    return high, middle, low


def left_stack(values, extra):
    h, m, l = (part.astype(f32) for part in split3(values))
    return jnp.concatenate([h, h, m, m, h, l] + extra, axis=0).astype(bf16)


def right_stack(values, extra):
    h, m, l = (part.astype(f32) for part in split3(values))
    return jnp.concatenate([h, m, h, m, l, h] + extra, axis=0).astype(bf16)


def eight_rows(rows, columns):
    index = lax.broadcasted_iota(jnp.int32, (8, columns), 0)
    out = jnp.zeros((8, columns), f32)
    for k, row in enumerate(rows):
        out = jnp.where(index == k, row, out)
    return [out, jnp.zeros((8, columns), f32)]


def three(values):
    return [part.astype(f32) for part in split3(values)]


def feature_tile(points, omega, phase, total):
    turn = 1.0 / (2.0 * math.pi)
    ones = [1.0] * 3
    left = left_stack(points, eight_rows(ones, points.shape[1]))
    right = right_stack(omega * turn, eight_rows(three(phase * turn), omega.shape[1]))
    turns = lax.dot_general(
        left.astype(f32).T.astype(bf16), right, (((1,), (0,)), ((), ())), preferred_element_type=f32
    )
    rest = turns - jnp.floor(turns + 0.5)
    square = rest * rest
    scale = math.sqrt(2.0 / total)
    value = jnp.full(square.shape, COS[-1] * scale, f32)
    for coefficient in COS[-2::-1]:
        value = value * square + coefficient * scale
    return value.astype(bf16)


def prior_kernel(which, x_ref, omega_ref, phase_ref, weights_ref, targets_ref, noise_ref, out_ref):
    half = weights_ref.shape[1]
    start = pl.multiple_of(which[0] * half, 128)
    feats = feature_tile(
        x_ref[...], omega_ref[:, pl.ds(start, half)], phase_ref[:, pl.ds(start, half)], omega_ref.shape[1]
    )
    prior = lax.dot_general(weights_ref[...], feats, (((1,), (1,)), ((), ())), preferred_element_type=f32)
    own = targets_ref[...] - noise_ref[...].T
    copies = out_ref.shape[1] // own.shape[1]
    lane = lax.broadcasted_iota(jnp.int32, out_ref.shape, 1)
    here = lane // own.shape[1] == which[0]
    out_ref[...] = jnp.where(here, jnp.concatenate([own] * copies, axis=1), 0.0) - prior


def pack_kernel(mine_ref, other_ref, x_ref, payload_ref):
    samples = mine_ref.shape[0]
    payload_ref[:samples, :] = mine_ref[...] + other_ref[...]
    payload_ref[samples:, :] = x_ref[...]


def cand_kernel(which, x_ref, omega_ref, phase_ref, mine_ref, other_ref, out_ref):
    half = mine_ref.shape[1]
    total = omega_ref.shape[1]
    here = pl.multiple_of(which[0] * half, 128)
    there = pl.multiple_of((1 - which[0]) * half, 128)
    out = None
    for start, weights in ((here, mine_ref), (there, other_ref)):
        feats = feature_tile(x_ref[...], omega_ref[:, pl.ds(start, half)], phase_ref[:, pl.ds(start, half)], total)
        part = lax.dot_general(feats, weights[...], (((1,), (1,)), ((), ())), preferred_element_type=f32)
        out = part if out is None else out + part
    out_ref[...] = out


def solve_kernel(
    own_rows, which, gathered_ref, cand_ref, prior_ref, samples_ref, solution_ref,
    field_ref, first_ref, rhs_ref, left_ref, right_ref, kernel_ref,
):
    blocks, _, width = gathered_ref.shape
    samples = prior_ref.shape[1]
    count = blocks * width
    points = []
    for k in range(blocks):
        columns = pl.ds(k * width, width)
        rhs_ref[:, columns] = gathered_ref[k, :samples, :]
        first_ref[:, columns] = gathered_ref[k, :samples, :].astype(bf16)
        points.append(gathered_ref[k, samples:, :])
    points = jnp.concatenate(points, axis=1)
    ones = [1.0] * 3
    halves = three((-0.5 * LOG2E) * jnp.sum(points * points, axis=0, keepdims=True))
    right_ref[...] = right_stack(points, eight_rows(ones + halves, count))
    left = left_stack(points * LOG2E, eight_rows(halves + ones, count))
    left_ref[...] = left.astype(f32).T.astype(bf16)

    size = min(256, count)
    wide = min(512, count)
    field_ref[...] = jnp.zeros_like(field_ref)

    def panel(i, carry):
        rows = pl.ds(pl.multiple_of(i * size, size), size)
        lhs = left_ref[rows, :]
        for j in range(0, count, wide):
            exponent = jnp.dot(lhs, right_ref[:, j : j + wide], preferred_element_type=f32)
            tile = jnp.exp2(exponent).astype(bf16)
            kernel_ref[rows, j : j + wide] = tile
            field_ref[:, j : j + wide] += jnp.dot(
                first_ref[:, rows], tile, preferred_element_type=f32
            )
        return carry

    lax.fori_loop(0, count // size, panel, 0)

    def total(values):
        return jnp.sum(values, axis=1, keepdims=True)

    start = rhs_ref[...]
    image = field_ref[...] + noise_level * start
    norm0 = total(start * start)
    alpha0 = norm0 / total(start * image)
    residual = start - alpha0 * image
    norm1 = total(residual * residual)
    beta = norm1 / norm0
    direction = residual + beta * start
    packed = direction.astype(bf16)
    second = jnp.dot(packed, kernel_ref[...], preferred_element_type=f32) + noise_level * direction
    alpha1 = norm1 / total(direction * second)
    field = alpha0 * start + alpha1 * direction
    weights = field.astype(bf16)
    own_solution = field[:, :width].T
    solution_ref[...] = jnp.where(which[0] == 0, own_solution[:own_rows], own_solution[own_rows:])

    cand = cand_ref[...]
    cand_halves = three((-0.5 * LOG2E) * jnp.sum(cand * cand, axis=0, keepdims=True))
    lhs = left_stack(cand * LOG2E, eight_rows(cand_halves + ones, cand.shape[1]))
    exponent = jnp.dot(lhs.astype(f32).T.astype(bf16), right_ref[...], preferred_element_type=f32)
    tile = jnp.exp2(exponent).astype(bf16)
    samples_ref[...] = prior_ref[...] + lax.dot_general(
        tile, weights, (((1,), (1,)), ((), ())), preferred_element_type=f32
    )


def call(kernel, out_shape, scratch=(), scalars=0, inputs=0, flops=0, transcendentals=0):
    vmem = pl.BlockSpec(memory_space=pltpu.VMEM)
    smem = pl.BlockSpec(memory_space=pltpu.SMEM)
    outs = jax.tree.map(lambda _: vmem, out_shape)
    return pl.pallas_call(
        kernel,
        out_shape=out_shape,
        in_specs=[smem] * scalars + [vmem] * inputs,
        out_specs=outs,
        scratch_shapes=list(scratch),
        cost_estimate=pl.CostEstimate(flops=flops, transcendentals=transcendentals, bytes_accessed=1 << 20),
        compiler_params=pltpu.CompilerParams(vmem_limit_bytes=48 << 20),
    )


def local_body(x_train, x_cand, targets, noise, omega, phase, prior_weights):
    own_rows, samples = noise.shape
    dim, width = x_train.shape
    blocks = lax.axis_size("train")
    count = blocks * width
    cand_index = lax.axis_index("cand")
    train_index = lax.axis_index("train")
    which = cand_index.astype(jnp.int32).reshape(1)
    phase = phase.reshape(1, -1)
    swap = [(0, 1), (1, 0)]
    weights = prior_weights.T
    partial = call(
        prior_kernel,
        jax.ShapeDtypeStruct((samples, width), f32),
        scalars=1, inputs=6, flops=1 << 30,
    )(which, x_train, omega, phase, weights, targets.reshape(1, -1), noise)
    other = lax.ppermute(partial, "cand", swap)
    payload = call(
        pack_kernel, jax.ShapeDtypeStruct((samples + dim, width), f32), inputs=3
    )(partial, other, x_train)
    payload, late_weights = lax.optimization_barrier((payload, weights))
    other_weights = lax.ppermute(late_weights, "cand", swap)
    gathered = payload[None]
    bit = blocks // 2
    while bit:
        moved = lax.ppermute(gathered, "train", [(i, i ^ bit) for i in range(blocks)])
        gathered = jnp.concatenate([gathered, moved], axis=0)
        bit //= 2
    per_device = x_cand.shape[1] // blocks
    mine = lax.dynamic_slice_in_dim(x_cand, train_index * per_device, per_device, 1)
    prior_cand = call(
        cand_kernel, jax.ShapeDtypeStruct((per_device, samples), f32), scalars=1, inputs=5, flops=1 << 30
    )(which, mine, omega, phase, weights, other_weights)
    stack = 6 * dim + 16
    return tuple(
        call(
            functools.partial(solve_kernel, own_rows),
            (
                jax.ShapeDtypeStruct((per_device, samples), f32),
                jax.ShapeDtypeStruct((own_rows, samples), f32),
            ),
            scratch=[
                pltpu.VMEM((samples, count), f32),
                pltpu.VMEM((samples, count), bf16),
                pltpu.VMEM((samples, count), f32),
                pltpu.VMEM((count, stack), bf16),
                pltpu.VMEM((stack, count), bf16),
                pltpu.VMEM((count, count), bf16),
            ],
            scalars=1, inputs=3, flops=1 << 34,
        )(which, gathered, mine, prior_cand)
    )


def is_local(mesh, x_train):
    train, cand = mesh.shape["train"], mesh.shape["cand"]
    count = x_train.shape[1]
    return cand == 2 and train & (train - 1) == 0 and 2 * count * count <= KERNEL_BYTES


def squares_of(points):
    return jnp.sum(points * points, axis=0)


def kernel_tile(row_points, row_norms, column_points, column_norms):
    inner = jnp.dot(row_points.T, column_points, precision=lax.Precision.HIGHEST)
    return jnp.exp(-0.5 * (row_norms[:, None] + column_norms[None, :] - 2.0 * inner)).astype(
        jnp.bfloat16
    )


def features(points, omega, phase):
    angles = jnp.dot(points.T, omega, precision=lax.Precision.HIGHEST) + phase[None, :]
    return (math.sqrt(2.0 / omega.shape[1]) * jnp.cos(angles)).astype(jnp.bfloat16)


def kernel_rows(points, every_point, every_norm, weights):
    count = points.shape[1]
    size = math.gcd(count, 1024)
    stacked = points.reshape(points.shape[0], count // size, size).transpose(1, 0, 2)

    def one_block(block_points):
        tile = kernel_tile(block_points, squares_of(block_points), every_point, every_norm)
        return jnp.dot(tile, weights, preferred_element_type=jnp.float32)

    return lax.map(one_block, stacked).reshape(count, weights.shape[1])


def body(x_train, x_cand, targets, noise, omega, phase, prior_weights):
    own_rows = noise.shape[0]
    cand_index = lax.axis_index("cand")
    train_index = lax.axis_index("train")
    own_points = lax.dynamic_slice_in_dim(x_train, cand_index * own_rows, own_rows, 1)
    full_weights = lax.all_gather(prior_weights, "cand", axis=0, tiled=True)
    prior_train = jnp.dot(
        features(own_points, omega, phase), full_weights, preferred_element_type=jnp.float32
    )
    rhs = targets[:, None] - prior_train - noise
    column_points = lax.all_gather(own_points, "train", axis=1, tiled=True)
    row_norms = squares_of(x_train)
    column_norms = squares_of(column_points)
    width = max(128, 262144 // x_train.shape[1])

    def squares(values):
        return lax.psum(jnp.sum(values * values, axis=0), ("train", "cand"))

    solution = jnp.zeros(rhs.shape, jnp.float32)
    residual = rhs
    direction = rhs
    norm_now = squares(residual)
    for step in range(ITERS):
        packed = direction.astype(jnp.bfloat16)
        empty = jnp.zeros((x_train.shape[1], packed.shape[1]), jnp.float32)
        total = empty
        piece = lax.all_gather(packed, "train", axis=0, tiled=True)
        for offset in range(0, piece.shape[0], width):
            count = min(width, piece.shape[0] - offset)
            accumulate_points = lax.dynamic_slice_in_dim(column_points, offset, count, 1)
            norms = lax.dynamic_slice_in_dim(column_norms, offset, count, 0)
            tile = kernel_tile(x_train, row_norms, accumulate_points, norms)
            total = total + jnp.dot(
                tile, piece[offset : offset + count], preferred_element_type=jnp.float32
            )
        apply_total = total
        apply_total = lax.psum_scatter(apply_total, "cand", scatter_dimension=0, tiled=True)
        image = apply_total + noise_level * direction
        curve = lax.psum(jnp.sum(direction * image, axis=0), ("train", "cand"))
        alpha = norm_now / curve
        solution = solution + alpha * direction
        residual = residual - alpha * image
        norm_next = squares(residual)
        direction = residual + norm_next / norm_now * direction
        norm_now = norm_next
    per_device = x_cand.shape[1] // lax.axis_size("train")
    mine = lax.dynamic_slice_in_dim(x_cand, train_index * per_device, per_device, 1)
    packed_solution = solution.astype(jnp.bfloat16)
    block_weights = lax.all_gather(packed_solution, "cand", axis=0, tiled=True)
    train_norms = squares_of(x_train)
    kernel_part = lax.psum_scatter(
        kernel_rows(x_cand, x_train, train_norms, block_weights),
        "train",
        scatter_dimension=0,
        tiled=True,
    )
    prior_cand = jnp.dot(
        features(mine, omega, phase), full_weights, preferred_element_type=jnp.float32
    )
    return (prior_cand + kernel_part, solution)


def solution(mesh):
    placed = (
        P(None, "train"),
        P(None, "cand"),
        P(("train", "cand")),
        P(("train", "cand"), None),
        P(),
        P(),
        P("cand", None),
    )
    def sharded(chosen):
        return jax.shard_map(
            chosen,
            mesh=mesh,
            in_specs=placed,
            out_specs=(P(("cand", "train"), None), P(("train", "cand"), None)),
            check_vma=False,
        )

    def step(x_train, *rest):
        chosen = local_body if is_local(mesh, x_train) else body
        return sharded(chosen)(x_train, *rest)

    return step
```

```python
import functools
import math

import jax
import jax.numpy as jnp
from jax import lax
from jax.experimental import pallas as pl
from jax.experimental.pallas import tpu as pltpu
from jax.sharding import PartitionSpec as P

ITERS = 2


noise_level = 0.5
LOG2E = math.log2(math.e)
COS = (
    1.0,
    -19.739208743087787,
    64.93938905249153,
    -85.45665775372363,
    60.24212493122888,
    -26.404630623401626,
    7.8000222194698186,
    -1.4529875517062139,
)
KERNEL_BYTES = 16 << 20
TILE = 256
f32, bf16 = jnp.float32, jnp.bfloat16


def split3(values):
    high = values.astype(bf16)
    rest = values - high.astype(f32)
    middle = rest.astype(bf16)
    low = (rest - middle.astype(f32)).astype(bf16)
    return high, middle, low


def left_stack(values, extra):
    h, m, l = (part.astype(f32) for part in split3(values))
    return jnp.concatenate([h, h, m, m, h, l] + extra, axis=0).astype(bf16)


def right_stack(values, extra):
    h, m, l = (part.astype(f32) for part in split3(values))
    return jnp.concatenate([h, m, h, m, l, h] + extra, axis=0).astype(bf16)


def eight_rows(rows, columns):
    index = lax.broadcasted_iota(jnp.int32, (8, columns), 0)
    out = jnp.zeros((8, columns), f32)
    for k, row in enumerate(rows):
        out = jnp.where(index == k, row, out)
    return [out, jnp.zeros((8, columns), f32)]


def three(values):
    return [part.astype(f32) for part in split3(values)]


def feature_tile(points, omega, phase, total):
    turn = 1.0 / (2.0 * math.pi)
    ones = [1.0] * 3
    left = left_stack(points, eight_rows(ones, points.shape[1]))
    right = right_stack(omega * turn, eight_rows(three(phase * turn), omega.shape[1]))
    turns = lax.dot_general(
        left.astype(f32).T.astype(bf16), right, (((1,), (0,)), ((), ())), preferred_element_type=f32
    )
    rest = turns - jnp.floor(turns + 0.5)
    square = rest * rest
    scale = math.sqrt(2.0 / total)
    value = jnp.full(square.shape, COS[-1] * scale, f32)
    for coefficient in COS[-2::-1]:
        value = value * square + coefficient * scale
    return value.astype(bf16)


def prior_kernel(
    which, x_hbm, omega_hbm, phase_hbm, weights_hbm, targets_hbm, noise_hbm, out_ref,
    x_ref, omega_ref, phase_ref, weights_ref, targets_ref, noise_ref, arrived,
):
    half = weights_hbm.shape[1]
    columns = pl.ds(pl.multiple_of(which[0] * half, 128), half)
    copies = [
        pltpu.make_async_copy(source, target, arrived.at[k])
        for k, (source, target) in enumerate((
            (x_hbm, x_ref),
            (omega_hbm.at[:, columns], omega_ref),
            (phase_hbm.at[:, columns], phase_ref),
            (weights_hbm, weights_ref),
            (targets_hbm, targets_ref),
            (noise_hbm, noise_ref),
        ))
    ]
    for copy in copies:
        copy.start()
    for copy in copies[:3]:
        copy.wait()
    feats = feature_tile(x_ref[...], omega_ref[...], phase_ref[...], omega_hbm.shape[1])
    for copy in copies[3:]:
        copy.wait()
    prior = lax.dot_general(weights_ref[...], feats, (((1,), (1,)), ((), ())), preferred_element_type=f32)
    own = targets_ref[...] - noise_ref[...].T
    repeats = out_ref.shape[1] // own.shape[1]
    lane = lax.broadcasted_iota(jnp.int32, out_ref.shape, 1)
    here = lane // own.shape[1] == which[0]
    out_ref[...] = jnp.where(here, jnp.concatenate([own] * repeats, axis=1), 0.0) - prior


def pack_kernel(mine_ref, other_ref, x_ref, pair_ref, payload_ref):
    samples, dim = mine_ref.shape[0], x_ref.shape[0]
    payload_ref[:samples, :] = mine_ref[...] + other_ref[...]
    payload_ref[samples : samples + dim, :] = x_ref[...]
    payload_ref[samples + dim :, :] = pair_ref[...]


def cand_kernel(which, x_ref, omega_ref, phase_ref, mine_ref, other_ref, out_ref):
    half = mine_ref.shape[1]
    total = omega_ref.shape[1]
    here = pl.multiple_of(which[0] * half, 128)
    there = pl.multiple_of((1 - which[0]) * half, 128)
    out = None
    for start, weights in ((here, mine_ref), (there, other_ref)):
        feats = feature_tile(x_ref[...], omega_ref[:, pl.ds(start, half)], phase_ref[:, pl.ds(start, half)], total)
        part = lax.dot_general(feats, weights[...], (((1,), (1,)), ((), ())), preferred_element_type=f32)
        out = part if out is None else out + part
    out_ref[...] = out


def halves_of(points):
    return three((-0.5 * LOG2E) * jnp.sum(points * points, axis=0, keepdims=True))


def left_of(points):
    stack = left_stack(points * LOG2E, eight_rows(halves_of(points) + [1.0] * 3, points.shape[1]))
    return stack.astype(f32).T.astype(bf16)


def right_of(points):
    return right_stack(points, eight_rows([1.0] * 3 + halves_of(points), points.shape[1]))


def fill(out_ref, left_ref, right_ref):
    rows, columns = out_ref.shape
    for i in range(0, rows, TILE):
        for j in range(0, columns, TILE):
            height, width = min(TILE, rows - i), min(TILE, columns - j)
            exponent = jnp.dot(
                left_ref[i : i + height, :], right_ref[:, j : j + width], preferred_element_type=f32
            )
            out_ref[i : i + height, j : j + width] = jnp.exp2(exponent).astype(bf16)


def points_of(block_ref, samples):
    dim = (block_ref.shape[1] - samples) // 2
    return jnp.concatenate(
        [block_ref[k, samples : samples + dim, :] for k in range(block_ref.shape[0])]
        + [block_ref[k, samples + dim :, :] for k in range(block_ref.shape[0])],
        axis=1,
    )


def rows_of(block_ref, samples, first=0, last=None):
    last = block_ref.shape[0] if last is None else last
    return jnp.concatenate([block_ref[k, :samples, :] for k in range(first, last)], axis=1)


def near_kernel(block_ref, cand_ref, left_ref, right_ref, cand_left_ref, kernel_ref, tile_ref):
    samples = block_ref.shape[1] - 2 * cand_ref.shape[0]
    points = points_of(block_ref, samples)
    left_ref[...] = left_of(points)
    right_ref[...] = right_of(points)
    cand_left_ref[...] = left_of(cand_ref[...])
    fill(kernel_ref, left_ref, right_ref)
    fill(tile_ref, cand_left_ref, right_ref)


def far_kernel(
    block_ref, near_ref, left_ref, right_ref, cand_left_ref, kernel_ref,
    near_far_ref, far_near_ref, far_far_ref, tile_ref, field_ref,
    far_left_ref, far_right_ref,
):
    samples = field_ref.shape[0]
    points = points_of(block_ref, samples)
    far_left_ref[...] = left_of(points)
    far_right_ref[...] = right_of(points)
    fill(near_far_ref, left_ref, far_right_ref)
    fill(far_near_ref, far_left_ref, right_ref)
    fill(far_far_ref, far_left_ref, far_right_ref)
    fill(tile_ref, cand_left_ref, far_right_ref)
    add_field(
        field_ref, None, slice(0, points.shape[1] // 2),
        rows_of(near_ref, samples).astype(bf16), rows_of(block_ref, samples).astype(bf16),
        kernel_ref, near_far_ref, far_near_ref, far_far_ref,
    )


def add_field(field_ref, before_ref, rows, near, far, near_near, near_far, far_near, far_far):
    count = near_near.shape[0]
    for j in range(0, count, TILE):
        for offset, first, second in ((0, near_near, far_near), (count, near_far, far_far)):
            width = min(TILE, count - j)
            columns = slice(offset + j, offset + j + width)
            value = jnp.dot(near, first[rows, j : j + width], preferred_element_type=f32)
            value += jnp.dot(far, second[rows, j : j + width], preferred_element_type=f32)
            if before_ref is not None:
                value += before_ref[:, columns]
            field_ref[:, columns] = value


def solve_kernel(
    own_rows, which, near_ref, far_ref, other_ref, before_ref,
    near_near_ref, near_far_ref, far_near_ref, far_far_ref,
    near_tile_ref, far_tile_ref, prior_ref, samples_ref, solution_ref,
    field_ref, start_ref, direction_ref, packed_ref,
):
    samples = prior_ref.shape[1]
    blocks, _, width = near_ref.shape
    half = blocks * width
    count = 2 * half
    near_other = rows_of(other_ref, samples, 0, blocks)
    far_other = rows_of(other_ref, samples, blocks, 2 * blocks)
    add_field(
        field_ref, before_ref, slice(half, count), near_other.astype(bf16), far_other.astype(bf16),
        near_near_ref, near_far_ref, far_near_ref, far_far_ref,
    )
    start_ref[:, :half] = rows_of(near_ref, samples)
    start_ref[:, half:count] = near_other
    start_ref[:, count : count + half] = rows_of(far_ref, samples)
    start_ref[:, count + half :] = far_other

    def total(values):
        return jnp.sum(values, axis=1, keepdims=True)

    start = start_ref[...]
    image = field_ref[...] + noise_level * start
    norm0 = total(start * start)
    alpha0 = norm0 / total(start * image)
    residual = start - alpha0 * image
    norm1 = total(residual * residual)
    direction = residual + (norm1 / norm0) * start
    direction_ref[...] = direction
    packed_ref[...] = direction.astype(bf16)

    curve = jnp.zeros((samples, min(TILE, count)), f32)
    for j in range(0, 2 * count, TILE):
        columns = slice(j, j + TILE)
        offset = j % count
        diagonal, above = (near_near_ref, None) if j < count else (far_far_ref, near_far_ref)
        value = jnp.zeros((samples, TILE), f32)
        if above is not None:
            value += jnp.dot(
                packed_ref[:, :count], above[:, offset : offset + TILE], preferred_element_type=f32
            )
        if offset:
            value += jnp.dot(
                packed_ref[:, j - offset : j], diagonal[:offset, offset : offset + TILE],
                preferred_element_type=f32,
            )
        value = 2.0 * value + jnp.dot(
            packed_ref[:, columns], diagonal[offset : offset + TILE, offset : offset + TILE],
            preferred_element_type=f32,
        )
        curve += direction_ref[:, columns] * (value + noise_level * direction_ref[:, columns])
    alpha1 = norm1 / total(curve)
    field = alpha0 * start_ref[...] + alpha1 * direction_ref[...]
    weights = field.astype(bf16)
    own_solution = field[:, :width].T
    solution_ref[...] = jnp.where(which[0] == 0, own_solution[:own_rows], own_solution[own_rows:])
    last = (((1,), (1,)), ((), ()))
    samples_ref[...] = (
        prior_ref[...]
        + lax.dot_general(near_tile_ref[...], weights[:, :count], last, preferred_element_type=f32)
        + lax.dot_general(far_tile_ref[...], weights[:, count:], last, preferred_element_type=f32)
    )


def call(kernel, out_shape, inputs, scratch=(), scalars=0, hbm=False, flops=0):
    vmem = pl.BlockSpec(memory_space=pltpu.VMEM)
    smem = pl.BlockSpec(memory_space=pltpu.SMEM)
    source = pl.BlockSpec(memory_space=pltpu.HBM) if hbm else vmem
    return pl.pallas_call(
        kernel,
        out_shape=out_shape,
        in_specs=[smem] * scalars + [source] * inputs,
        out_specs=jax.tree.map(lambda _: vmem, out_shape),
        scratch_shapes=list(scratch),
        cost_estimate=pl.CostEstimate(flops=flops, transcendentals=0, bytes_accessed=1 << 20),
        compiler_params=pltpu.CompilerParams(vmem_limit_bytes=16 << 20),
    )


def local_body(x_train, x_cand, targets, noise, omega, phase, prior_weights):
    own_rows, samples = noise.shape
    dim, width = x_train.shape
    blocks = lax.axis_size("train")
    cand_index = lax.axis_index("cand")
    train_index = lax.axis_index("train")
    which = cand_index.astype(jnp.int32).reshape(1)
    phase = phase.reshape(1, -1)
    weights = prior_weights.T
    half_features = weights.shape[1]
    shape = jax.ShapeDtypeStruct
    swap = [(0, 1), (1, 0)]

    def in_hbm(values):
        return pltpu.with_memory_space_constraint(values, pltpu.HBM)

    def exchange(values, bit):
        return lax.ppermute(values, "train", [(i, i ^ bit) for i in range(blocks)])

    pair = exchange(x_train, 1)
    partial = call(
        prior_kernel,
        shape((samples, width), f32),
        scalars=1, inputs=6, hbm=True, flops=1 << 30,
        scratch=[
            pltpu.VMEM((dim, width), f32),
            pltpu.VMEM((dim, half_features), f32),
            pltpu.VMEM((1, half_features), f32),
            pltpu.VMEM(weights.shape, bf16),
            pltpu.VMEM((1, own_rows), f32),
            pltpu.VMEM(noise.shape, f32),
            pltpu.SemaphoreType.DMA((6,)),
        ],
    )(which, *map(in_hbm, (x_train, omega, phase, weights, targets.reshape(1, -1), noise)))
    other = lax.ppermute(partial, "cand", swap)
    payload = call(pack_kernel, shape((samples + 2 * dim, width), f32), inputs=4)(
        partial, other, x_train, pair
    )
    payload, late_weights = lax.optimization_barrier((payload, weights))
    other_weights = lax.ppermute(late_weights, "cand", swap)
    near = payload[None]
    bit = blocks // 2
    while bit > 2:
        near = jnp.concatenate([near, exchange(near, bit)], axis=0)
        bit //= 2
    far = exchange(near, 2)
    per_device = x_cand.shape[1] // blocks
    mine = lax.dynamic_slice_in_dim(x_cand, train_index * per_device, per_device, 1)
    prior_cand = call(cand_kernel, shape((per_device, samples), f32), scalars=1, inputs=5, flops=1 << 30)(
        which, mine, omega, phase, weights, other_weights
    )
    count = blocks * width // 2
    stack = 6 * dim + 16
    left, right, cand_left, near_near, near_tile = call(
        near_kernel,
        (
            shape((count, stack), bf16),
            shape((stack, count), bf16),
            shape((per_device, stack), bf16),
            shape((count, count), bf16),
            shape((per_device, count), bf16),
        ),
        inputs=2, flops=1 << 31,
    )(near, mine)
    other = exchange(jnp.concatenate([near[:, :samples], far[:, :samples]], axis=0), 1)
    near_far, far_near, far_far, far_tile, before = call(
        far_kernel,
        (
            shape((count, count), bf16),
            shape((count, count), bf16),
            shape((count, count), bf16),
            shape((per_device, count), bf16),
            shape((samples, 2 * count), f32),
        ),
        scratch=[pltpu.VMEM((count, stack), bf16), pltpu.VMEM((stack, count), bf16)],
        inputs=6, flops=1 << 33,
    )(far, near, left, right, cand_left, near_near)
    return tuple(
        call(
            functools.partial(solve_kernel, own_rows),
            (shape((per_device, samples), f32), shape((own_rows, samples), f32)),
            scratch=[
                pltpu.VMEM((samples, 2 * count), f32),
                pltpu.VMEM((samples, 2 * count), f32),
                pltpu.VMEM((samples, 2 * count), f32),
                pltpu.VMEM((samples, 2 * count), bf16),
            ],
            scalars=1, inputs=11, flops=1 << 33,
        )(
            which, near, far, other, before, near_near, near_far, far_near, far_far,
            near_tile, far_tile, prior_cand,
        )
    )


def is_local(mesh, x_train):
    train, cand = mesh.shape["train"], mesh.shape["cand"]
    count = x_train.shape[1]
    tiles = count // 2 % TILE == 0
    return cand == 2 and train >= 4 and train & (train - 1) == 0 and tiles and 2 * count * count <= KERNEL_BYTES


def squares_of(points):
    return jnp.sum(points * points, axis=0)


def kernel_tile(row_points, row_norms, column_points, column_norms):
    inner = jnp.dot(row_points.T, column_points, precision=lax.Precision.HIGHEST)
    return jnp.exp(-0.5 * (row_norms[:, None] + column_norms[None, :] - 2.0 * inner)).astype(
        jnp.bfloat16
    )


def features(points, omega, phase):
    angles = jnp.dot(points.T, omega, precision=lax.Precision.HIGHEST) + phase[None, :]
    return (math.sqrt(2.0 / omega.shape[1]) * jnp.cos(angles)).astype(jnp.bfloat16)


def kernel_rows(points, every_point, every_norm, weights):
    count = points.shape[1]
    size = math.gcd(count, 1024)
    stacked = points.reshape(points.shape[0], count // size, size).transpose(1, 0, 2)

    def one_block(block_points):
        tile = kernel_tile(block_points, squares_of(block_points), every_point, every_norm)
        return jnp.dot(tile, weights, preferred_element_type=jnp.float32)

    return lax.map(one_block, stacked).reshape(count, weights.shape[1])


def body(x_train, x_cand, targets, noise, omega, phase, prior_weights):
    own_rows = noise.shape[0]
    cand_index = lax.axis_index("cand")
    train_index = lax.axis_index("train")
    own_points = lax.dynamic_slice_in_dim(x_train, cand_index * own_rows, own_rows, 1)
    full_weights = lax.all_gather(prior_weights, "cand", axis=0, tiled=True)
    prior_train = jnp.dot(
        features(own_points, omega, phase), full_weights, preferred_element_type=jnp.float32
    )
    rhs = targets[:, None] - prior_train - noise
    column_points = lax.all_gather(own_points, "train", axis=1, tiled=True)
    row_norms = squares_of(x_train)
    column_norms = squares_of(column_points)
    width = max(128, 262144 // x_train.shape[1])

    def squares(values):
        return lax.psum(jnp.sum(values * values, axis=0), ("train", "cand"))

    solution = jnp.zeros(rhs.shape, jnp.float32)
    residual = rhs
    direction = rhs
    norm_now = squares(residual)
    for step in range(ITERS):
        packed = direction.astype(jnp.bfloat16)
        empty = jnp.zeros((x_train.shape[1], packed.shape[1]), jnp.float32)
        total = empty
        piece = lax.all_gather(packed, "train", axis=0, tiled=True)
        for offset in range(0, piece.shape[0], width):
            count = min(width, piece.shape[0] - offset)
            accumulate_points = lax.dynamic_slice_in_dim(column_points, offset, count, 1)
            norms = lax.dynamic_slice_in_dim(column_norms, offset, count, 0)
            tile = kernel_tile(x_train, row_norms, accumulate_points, norms)
            total = total + jnp.dot(
                tile, piece[offset : offset + count], preferred_element_type=jnp.float32
            )
        apply_total = total
        apply_total = lax.psum_scatter(apply_total, "cand", scatter_dimension=0, tiled=True)
        image = apply_total + noise_level * direction
        curve = lax.psum(jnp.sum(direction * image, axis=0), ("train", "cand"))
        alpha = norm_now / curve
        solution = solution + alpha * direction
        residual = residual - alpha * image
        norm_next = squares(residual)
        direction = residual + norm_next / norm_now * direction
        norm_now = norm_next
    per_device = x_cand.shape[1] // lax.axis_size("train")
    mine = lax.dynamic_slice_in_dim(x_cand, train_index * per_device, per_device, 1)
    packed_solution = solution.astype(jnp.bfloat16)
    block_weights = lax.all_gather(packed_solution, "cand", axis=0, tiled=True)
    train_norms = squares_of(x_train)
    kernel_part = lax.psum_scatter(
        kernel_rows(x_cand, x_train, train_norms, block_weights),
        "train",
        scatter_dimension=0,
        tiled=True,
    )
    prior_cand = jnp.dot(
        features(mine, omega, phase), full_weights, preferred_element_type=jnp.float32
    )
    return (prior_cand + kernel_part, solution)


def solution(mesh):
    placed = (
        P(None, "train"),
        P(None, "cand"),
        P(("train", "cand")),
        P(("train", "cand"), None),
        P(),
        P(),
        P("cand", None),
    )
    def sharded(chosen):
        return jax.shard_map(
            chosen,
            mesh=mesh,
            in_specs=placed,
            out_specs=(P(("cand", "train"), None), P(("train", "cand"), None)),
            check_vma=False,
        )

    def step(x_train, *rest):
        chosen = local_body if is_local(mesh, x_train) else body
        return sharded(chosen)(x_train, *rest)

    return step
```

```python
import functools
import math

import jax
import jax.numpy as jnp
from jax import lax
from jax.experimental import pallas as pl
from jax.experimental.pallas import tpu as pltpu
from jax.sharding import PartitionSpec as P

ITERS = 2


noise_level = 0.5
LOG2E = math.log2(math.e)
COS = (
    1.0,
    -19.739208743087787,
    64.93938905249153,
    -85.45665775372363,
    60.24212493122888,
    -26.404630623401626,
    7.8000222194698186,
    -1.4529875517062139,
)
KERNEL_BYTES = 16 << 20
TILE = 256
f32, bf16 = jnp.float32, jnp.bfloat16


def split3(values):
    high = values.astype(bf16)
    rest = values - high.astype(f32)
    middle = rest.astype(bf16)
    low = (rest - middle.astype(f32)).astype(bf16)
    return high, middle, low


def left_stack(values, extra):
    h, m, l = (part.astype(f32) for part in split3(values))
    return jnp.concatenate([h, h, m, m, h, l] + extra, axis=0).astype(bf16)


def right_stack(values, extra):
    h, m, l = (part.astype(f32) for part in split3(values))
    return jnp.concatenate([h, m, h, m, l, h] + extra, axis=0).astype(bf16)


def eight_rows(rows, columns):
    index = lax.broadcasted_iota(jnp.int32, (8, columns), 0)
    out = jnp.zeros((8, columns), f32)
    for k, row in enumerate(rows):
        out = jnp.where(index == k, row, out)
    return [out, jnp.zeros((8, columns), f32)]


def three(values):
    return [part.astype(f32) for part in split3(values)]


def feature_tile(points, omega, phase, total):
    turn = 1.0 / (2.0 * math.pi)
    ones = [1.0] * 3
    left = left_stack(points, eight_rows(ones, points.shape[1]))
    right = right_stack(omega * turn, eight_rows(three(phase * turn), omega.shape[1]))
    turns = lax.dot_general(
        left.astype(f32).T.astype(bf16), right, (((1,), (0,)), ((), ())), preferred_element_type=f32
    )
    rest = turns - jnp.floor(turns + 0.5)
    square = rest * rest
    scale = math.sqrt(2.0 / total)
    value = jnp.full(square.shape, COS[-1] * scale, f32)
    for coefficient in COS[-2::-1]:
        value = value * square + coefficient * scale
    return value.astype(bf16)


def prior_kernel(
    which, x_hbm, omega_hbm, phase_hbm, weights_hbm, targets_hbm, noise_hbm, out_ref,
    x_ref, omega_ref, phase_ref, weights_ref, targets_ref, noise_ref, arrived,
):
    half = weights_hbm.shape[1]
    columns = pl.ds(pl.multiple_of(which[0] * half, 128), half)
    copies = [
        pltpu.make_async_copy(source, target, arrived.at[k])
        for k, (source, target) in enumerate((
            (x_hbm, x_ref),
            (omega_hbm.at[:, columns], omega_ref),
            (phase_hbm.at[:, columns], phase_ref),
            (weights_hbm, weights_ref),
            (targets_hbm, targets_ref),
            (noise_hbm, noise_ref),
        ))
    ]
    for copy in copies:
        copy.start()
    for copy in copies[:3]:
        copy.wait()
    feats = feature_tile(x_ref[...], omega_ref[...], phase_ref[...], omega_hbm.shape[1])
    for copy in copies[3:]:
        copy.wait()
    prior = lax.dot_general(weights_ref[...], feats, (((1,), (1,)), ((), ())), preferred_element_type=f32)
    own = targets_ref[...] - noise_ref[...].T
    repeats = out_ref.shape[1] // own.shape[1]
    lane = lax.broadcasted_iota(jnp.int32, out_ref.shape, 1)
    here = lane // own.shape[1] == which[0]
    out_ref[...] = jnp.where(here, jnp.concatenate([own] * repeats, axis=1), 0.0) - prior


def pack_kernel(mine_ref, other_ref, x_ref, pair_ref, payload_ref):
    samples, dim = mine_ref.shape[0], x_ref.shape[0]
    payload_ref[:samples, :] = mine_ref[...] + other_ref[...]
    payload_ref[samples : samples + dim, :] = x_ref[...]
    payload_ref[samples + dim :, :] = pair_ref[...]


def cand_kernel(which, x_ref, omega_ref, phase_ref, mine_ref, other_ref, out_ref):
    half = mine_ref.shape[1]
    total = omega_ref.shape[1]
    here = pl.multiple_of(which[0] * half, 128)
    there = pl.multiple_of((1 - which[0]) * half, 128)
    out = None
    for start, weights in ((here, mine_ref), (there, other_ref)):
        feats = feature_tile(x_ref[...], omega_ref[:, pl.ds(start, half)], phase_ref[:, pl.ds(start, half)], total)
        part = lax.dot_general(feats, weights[...], (((1,), (1,)), ((), ())), preferred_element_type=f32)
        out = part if out is None else out + part
    out_ref[...] = out


def halves_of(points):
    return three((-0.5 * LOG2E) * jnp.sum(points * points, axis=0, keepdims=True))


def left_of(points):
    stack = left_stack(points * LOG2E, eight_rows(halves_of(points) + [1.0] * 3, points.shape[1]))
    return stack.astype(f32).T.astype(bf16)


def right_of(points):
    return right_stack(points, eight_rows([1.0] * 3 + halves_of(points), points.shape[1]))


def fill(out_ref, left_ref, right_ref):
    rows, columns = out_ref.shape
    for i in range(0, rows, TILE):
        for j in range(0, columns, TILE):
            height, width = min(TILE, rows - i), min(TILE, columns - j)
            exponent = jnp.dot(
                left_ref[i : i + height, :], right_ref[:, j : j + width], preferred_element_type=f32
            )
            out_ref[i : i + height, j : j + width] = jnp.exp2(exponent).astype(bf16)


def points_of(block_ref, samples):
    dim = (block_ref.shape[1] - samples) // 2
    return jnp.concatenate(
        [block_ref[k, samples : samples + dim, :] for k in range(block_ref.shape[0])]
        + [block_ref[k, samples + dim :, :] for k in range(block_ref.shape[0])],
        axis=1,
    )


def rows_of(block_ref, samples, first=0, last=None):
    last = block_ref.shape[0] if last is None else last
    return jnp.concatenate([block_ref[k, :samples, :] for k in range(first, last)], axis=1)


def product(rows, kernel):
    return jnp.dot(rows, kernel, preferred_element_type=f32)


def product_transposed(rows, kernel):
    return lax.dot_general(rows, kernel, (((1,), (1,)), ((), ())), preferred_element_type=f32)


def near_kernel(
    block_ref, cand_ref, left_ref, right_ref, cand_left_ref, kernel_ref, tile_ref, field_ref
):
    samples = field_ref.shape[0]
    points = points_of(block_ref, samples)
    left_ref[...] = left_of(points)
    right_ref[...] = right_of(points)
    cand_left_ref[...] = left_of(cand_ref[...])
    fill(kernel_ref, left_ref, right_ref)
    fill(tile_ref, cand_left_ref, right_ref)
    half = points.shape[1] // 2
    field_ref[...] = product(rows_of(block_ref, samples).astype(bf16), kernel_ref[:half, :])


def far_kernel(
    block_ref, near_ref, left_ref, right_ref, cand_left_ref, before_ref,
    near_far_ref, far_far_ref, tile_ref, field_ref,
    far_left_ref, far_right_ref,
):
    samples = field_ref.shape[0]
    points = points_of(block_ref, samples)
    far_left_ref[...] = left_of(points)
    far_right_ref[...] = right_of(points)
    fill(near_far_ref, left_ref, far_right_ref)
    fill(far_far_ref, far_left_ref, far_right_ref)
    fill(tile_ref, cand_left_ref, far_right_ref)
    half, count = points.shape[1] // 2, points.shape[1]
    near, far = rows_of(near_ref, samples).astype(bf16), rows_of(block_ref, samples).astype(bf16)
    field_ref[:, :count] = before_ref[...] + product_transposed(far, near_far_ref[:, :half])
    field_ref[:, count:] = product(near, near_far_ref[:half, :]) + product(far, far_far_ref[:half, :])


def solve_kernel(
    own_rows, which, near_ref, far_ref, other_ref, before_ref,
    near_near_ref, near_far_ref, far_far_ref,
    near_tile_ref, far_tile_ref, prior_ref, samples_ref, solution_ref,
    field_ref, start_ref, direction_ref, packed_ref,
):
    samples = prior_ref.shape[1]
    blocks, _, width = near_ref.shape
    half = blocks * width
    count = 2 * half
    near_other = rows_of(other_ref, samples, 0, blocks)
    far_other = rows_of(other_ref, samples, blocks, 2 * blocks)
    near, far = near_other.astype(bf16), far_other.astype(bf16)
    field_ref[:, :count] = (
        before_ref[:, :count]
        + product(near, near_near_ref[half:, :])
        + product_transposed(far, near_far_ref[:, half:])
    )
    field_ref[:, count:] = (
        before_ref[:, count:] + product(near, near_far_ref[half:, :]) + product(far, far_far_ref[half:, :])
    )
    start_ref[:, :half] = rows_of(near_ref, samples)
    start_ref[:, half:count] = near_other
    start_ref[:, count : count + half] = rows_of(far_ref, samples)
    start_ref[:, count + half :] = far_other

    def total(values):
        return jnp.sum(values, axis=1, keepdims=True)

    start = start_ref[...]
    image = field_ref[...] + noise_level * start
    norm0 = total(start * start)
    alpha0 = norm0 / total(start * image)
    residual = start - alpha0 * image
    norm1 = total(residual * residual)
    direction = residual + (norm1 / norm0) * start
    direction_ref[...] = direction
    packed_ref[...] = direction.astype(bf16)

    curve = jnp.zeros((samples, min(TILE, count)), f32)
    for j in range(0, 2 * count, TILE):
        columns = slice(j, j + TILE)
        offset = j % count
        diagonal, above = (near_near_ref, None) if j < count else (far_far_ref, near_far_ref)
        value = jnp.zeros((samples, TILE), f32)
        if above is not None:
            value += jnp.dot(
                packed_ref[:, :count], above[:, offset : offset + TILE], preferred_element_type=f32
            )
        if offset:
            value += jnp.dot(
                packed_ref[:, j - offset : j], diagonal[:offset, offset : offset + TILE],
                preferred_element_type=f32,
            )
        value = 2.0 * value + jnp.dot(
            packed_ref[:, columns], diagonal[offset : offset + TILE, offset : offset + TILE],
            preferred_element_type=f32,
        )
        curve += direction_ref[:, columns] * (value + noise_level * direction_ref[:, columns])
    alpha1 = norm1 / total(curve)
    field = alpha0 * start_ref[...] + alpha1 * direction_ref[...]
    weights = field.astype(bf16)
    own_solution = field[:, :width].T
    solution_ref[...] = jnp.where(which[0] == 0, own_solution[:own_rows], own_solution[own_rows:])
    last = (((1,), (1,)), ((), ()))
    samples_ref[...] = (
        prior_ref[...]
        + lax.dot_general(near_tile_ref[...], weights[:, :count], last, preferred_element_type=f32)
        + lax.dot_general(far_tile_ref[...], weights[:, count:], last, preferred_element_type=f32)
    )


def call(kernel, out_shape, inputs, scratch=(), scalars=0, hbm=False, flops=0):
    vmem = pl.BlockSpec(memory_space=pltpu.VMEM)
    smem = pl.BlockSpec(memory_space=pltpu.SMEM)
    source = pl.BlockSpec(memory_space=pltpu.HBM) if hbm else vmem
    return pl.pallas_call(
        kernel,
        out_shape=out_shape,
        in_specs=[smem] * scalars + [source] * inputs,
        out_specs=jax.tree.map(lambda _: vmem, out_shape),
        scratch_shapes=list(scratch),
        cost_estimate=pl.CostEstimate(flops=flops, transcendentals=0, bytes_accessed=1 << 20),
        compiler_params=pltpu.CompilerParams(vmem_limit_bytes=16 << 20),
    )


def local_body(x_train, x_cand, targets, noise, omega, phase, prior_weights):
    own_rows, samples = noise.shape
    dim, width = x_train.shape
    blocks = lax.axis_size("train")
    cand_index = lax.axis_index("cand")
    train_index = lax.axis_index("train")
    which = cand_index.astype(jnp.int32).reshape(1)
    phase = phase.reshape(1, -1)
    weights = prior_weights.T
    half_features = weights.shape[1]
    shape = jax.ShapeDtypeStruct
    swap = [(0, 1), (1, 0)]

    def in_hbm(values):
        return pltpu.with_memory_space_constraint(values, pltpu.HBM)

    def exchange(values, bit):
        return lax.ppermute(values, "train", [(i, i ^ bit) for i in range(blocks)])

    pair = exchange(x_train, 1)
    partial = call(
        prior_kernel,
        shape((samples, width), f32),
        scalars=1, inputs=6, hbm=True, flops=1 << 30,
        scratch=[
            pltpu.VMEM((dim, width), f32),
            pltpu.VMEM((dim, half_features), f32),
            pltpu.VMEM((1, half_features), f32),
            pltpu.VMEM(weights.shape, bf16),
            pltpu.VMEM((1, own_rows), f32),
            pltpu.VMEM(noise.shape, f32),
            pltpu.SemaphoreType.DMA((6,)),
        ],
    )(which, *map(in_hbm, (x_train, omega, phase, weights, targets.reshape(1, -1), noise)))
    other = lax.ppermute(partial, "cand", swap)
    payload = call(pack_kernel, shape((samples + 2 * dim, width), f32), inputs=4)(
        partial, other, x_train, pair
    )
    other_weights = lax.ppermute(weights, "cand", swap)
    first = payload[None]
    bit = blocks // 2
    while bit > 4:
        first = jnp.concatenate([first, exchange(first, bit)], axis=0)
        bit //= 2
    third = exchange(first, 6)
    second = exchange(first, 4)
    near = jnp.concatenate([first, exchange(first, 2)], axis=0)
    far = jnp.concatenate([second, third], axis=0)
    per_device = x_cand.shape[1] // blocks
    mine = lax.dynamic_slice_in_dim(x_cand, train_index * per_device, per_device, 1)
    prior_cand = call(cand_kernel, shape((per_device, samples), f32), scalars=1, inputs=5, flops=1 << 30)(
        which, mine, omega, phase, weights, other_weights
    )
    count = blocks * width // 2
    stack = 6 * dim + 16
    square = shape((count, count), bf16)
    left, right, cand_left, near_near, near_tile, before = call(
        near_kernel,
        (
            shape((count, stack), bf16),
            shape((stack, count), bf16),
            shape((per_device, stack), bf16),
            square,
            shape((per_device, count), bf16),
            shape((samples, count), f32),
        ),
        inputs=2, flops=1 << 31,
    )(near, mine)
    other = exchange(jnp.concatenate([near[:, :samples], far[:, :samples]], axis=0), 1)
    near_far, far_far, far_tile, before = call(
        far_kernel,
        (square, square, shape((per_device, count), bf16), shape((samples, 2 * count), f32)),
        scratch=[pltpu.VMEM((count, stack), bf16), pltpu.VMEM((stack, count), bf16)],
        inputs=6, flops=1 << 33,
    )(far, near, left, right, cand_left, before)
    return tuple(
        call(
            functools.partial(solve_kernel, own_rows),
            (shape((per_device, samples), f32), shape((own_rows, samples), f32)),
            scratch=[
                pltpu.VMEM((samples, 2 * count), f32),
                pltpu.VMEM((samples, 2 * count), f32),
                pltpu.VMEM((samples, 2 * count), f32),
                pltpu.VMEM((samples, 2 * count), bf16),
            ],
            scalars=1, inputs=10, flops=1 << 33,
        )(
            which, near, far, other, before, near_near, near_far, far_far,
            near_tile, far_tile, prior_cand,
        )
    )


def is_local(mesh, x_train):
    train, cand = mesh.shape["train"], mesh.shape["cand"]
    count = x_train.shape[1]
    tiles = count // 2 % TILE == 0
    return cand == 2 and train >= 8 and train & (train - 1) == 0 and tiles and 2 * count * count <= KERNEL_BYTES


def squares_of(points):
    return jnp.sum(points * points, axis=0)


def kernel_tile(row_points, row_norms, column_points, column_norms):
    inner = jnp.dot(row_points.T, column_points, precision=lax.Precision.HIGHEST)
    return jnp.exp(-0.5 * (row_norms[:, None] + column_norms[None, :] - 2.0 * inner)).astype(
        jnp.bfloat16
    )


def features(points, omega, phase):
    angles = jnp.dot(points.T, omega, precision=lax.Precision.HIGHEST) + phase[None, :]
    return (math.sqrt(2.0 / omega.shape[1]) * jnp.cos(angles)).astype(jnp.bfloat16)


def kernel_rows(points, every_point, every_norm, weights):
    count = points.shape[1]
    size = math.gcd(count, 1024)
    stacked = points.reshape(points.shape[0], count // size, size).transpose(1, 0, 2)

    def one_block(block_points):
        tile = kernel_tile(block_points, squares_of(block_points), every_point, every_norm)
        return jnp.dot(tile, weights, preferred_element_type=jnp.float32)

    return lax.map(one_block, stacked).reshape(count, weights.shape[1])


def body(x_train, x_cand, targets, noise, omega, phase, prior_weights):
    own_rows = noise.shape[0]
    cand_index = lax.axis_index("cand")
    train_index = lax.axis_index("train")
    own_points = lax.dynamic_slice_in_dim(x_train, cand_index * own_rows, own_rows, 1)
    full_weights = lax.all_gather(prior_weights, "cand", axis=0, tiled=True)
    prior_train = jnp.dot(
        features(own_points, omega, phase), full_weights, preferred_element_type=jnp.float32
    )
    rhs = targets[:, None] - prior_train - noise
    column_points = lax.all_gather(own_points, "train", axis=1, tiled=True)
    row_norms = squares_of(x_train)
    column_norms = squares_of(column_points)
    width = max(128, 262144 // x_train.shape[1])

    def squares(values):
        return lax.psum(jnp.sum(values * values, axis=0), ("train", "cand"))

    solution = jnp.zeros(rhs.shape, jnp.float32)
    residual = rhs
    direction = rhs
    norm_now = squares(residual)
    for _ in range(ITERS):
        packed = direction.astype(jnp.bfloat16)
        empty = jnp.zeros((x_train.shape[1], packed.shape[1]), jnp.float32)
        total = empty
        piece = lax.all_gather(packed, "train", axis=0, tiled=True)
        for offset in range(0, piece.shape[0], width):
            count = min(width, piece.shape[0] - offset)
            accumulate_points = lax.dynamic_slice_in_dim(column_points, offset, count, 1)
            norms = lax.dynamic_slice_in_dim(column_norms, offset, count, 0)
            tile = kernel_tile(x_train, row_norms, accumulate_points, norms)
            total = total + jnp.dot(
                tile, piece[offset : offset + count], preferred_element_type=jnp.float32
            )
        apply_total = total
        apply_total = lax.psum_scatter(apply_total, "cand", scatter_dimension=0, tiled=True)
        image = apply_total + noise_level * direction
        curve = lax.psum(jnp.sum(direction * image, axis=0), ("train", "cand"))
        alpha = norm_now / curve
        solution = solution + alpha * direction
        residual = residual - alpha * image
        norm_next = squares(residual)
        direction = residual + norm_next / norm_now * direction
        norm_now = norm_next
    per_device = x_cand.shape[1] // lax.axis_size("train")
    mine = lax.dynamic_slice_in_dim(x_cand, train_index * per_device, per_device, 1)
    packed_solution = solution.astype(jnp.bfloat16)
    block_weights = lax.all_gather(packed_solution, "cand", axis=0, tiled=True)
    train_norms = squares_of(x_train)
    kernel_part = lax.psum_scatter(
        kernel_rows(x_cand, x_train, train_norms, block_weights),
        "train",
        scatter_dimension=0,
        tiled=True,
    )
    prior_cand = jnp.dot(
        features(mine, omega, phase), full_weights, preferred_element_type=jnp.float32
    )
    return (prior_cand + kernel_part, solution)


def solution(mesh):
    placed = (
        P(None, "train"),
        P(None, "cand"),
        P(("train", "cand")),
        P(("train", "cand"), None),
        P(),
        P(),
        P("cand", None),
    )

    def sharded(chosen):
        return jax.shard_map(
            chosen,
            mesh=mesh,
            in_specs=placed,
            out_specs=(P(("cand", "train"), None), P(("train", "cand"), None)),
            check_vma=False,
        )

    def step(x_train, *rest):
        if not is_local(mesh, x_train):
            return sharded(body)(x_train, *rest)
        return sharded(local_body)(x_train, *rest)

    return step
```

```python
import functools
import math

import jax
import jax.numpy as jnp
from jax import lax
from jax.experimental import pallas as pl
from jax.experimental.pallas import tpu as pltpu
from jax.sharding import PartitionSpec as P

ITERS = 2


noise_level = 0.5
LOG2E = math.log2(math.e)
COS = (
    1.0,
    -19.739204466576105,
    64.93911592834385,
    -85.4501134274465,
    60.16742979141158,
    -25.96688461044869,
    6.527705959852582,
)
KERNEL_BYTES = 16 << 20
TILE = 256
f32, bf16 = jnp.float32, jnp.bfloat16


def split3(values):
    high = values.astype(bf16)
    rest = values - high.astype(f32)
    middle = rest.astype(bf16)
    low = (rest - middle.astype(f32)).astype(bf16)
    return high, middle, low


def left_stack(values, extra):
    h, m, l = (part.astype(f32) for part in split3(values))
    return jnp.concatenate([h, h, m, m, h, l] + extra, axis=0).astype(bf16)


def right_stack(values, extra):
    h, m, l = (part.astype(f32) for part in split3(values))
    return jnp.concatenate([h, m, h, m, l, h] + extra, axis=0).astype(bf16)


def eight_rows(rows, columns):
    index = lax.broadcasted_iota(jnp.int32, (8, columns), 0)
    out = jnp.zeros((8, columns), f32)
    for k, row in enumerate(rows):
        out = jnp.where(index == k, row, out)
    return [out, jnp.zeros((8, columns), f32)]


def three(values):
    return [part.astype(f32) for part in split3(values)]


def feature_tile(points, omega, phase, total):
    turn = 1.0 / (2.0 * math.pi)
    ones = [1.0] * 3
    left = left_stack(points, eight_rows(ones, points.shape[1]))
    right = right_stack(omega * turn, eight_rows(three(phase * turn), omega.shape[1]))
    turns = lax.dot_general(
        left.astype(f32).T.astype(bf16), right, (((1,), (0,)), ((), ())), preferred_element_type=f32
    )
    rest = turns - jnp.round(turns)
    square = rest * rest
    scale = math.sqrt(2.0 / total)
    value = jnp.full(square.shape, COS[-1] * scale, f32)
    for coefficient in COS[-2::-1]:
        value = value * square + coefficient * scale
    return value.astype(bf16)


def prior_kernel(
    which, x_hbm, omega_hbm, phase_hbm, weights_hbm, targets_hbm, noise_hbm, out_ref,
    x_ref, omega_ref, phase_ref, weights_ref, targets_ref, noise_ref, arrived,
):
    half = weights_hbm.shape[1]
    columns = pl.ds(pl.multiple_of(which[0] * half, 128), half)
    copies = [
        pltpu.make_async_copy(source, target, arrived.at[k])
        for k, (source, target) in enumerate((
            (x_hbm, x_ref),
            (omega_hbm.at[:, columns], omega_ref),
            (phase_hbm.at[:, columns], phase_ref),
            (weights_hbm, weights_ref),
            (targets_hbm, targets_ref),
            (noise_hbm, noise_ref),
        ))
    ]
    for copy in copies:
        copy.start()
    for copy in copies[:3]:
        copy.wait()
    feats = feature_tile(x_ref[...], omega_ref[...], phase_ref[...], omega_hbm.shape[1])
    for copy in copies[3:]:
        copy.wait()
    prior = lax.dot_general(weights_ref[...], feats, (((1,), (1,)), ((), ())), preferred_element_type=f32)
    own = targets_ref[...] - noise_ref[...].T
    repeats = out_ref.shape[1] // own.shape[1]
    lane = lax.broadcasted_iota(jnp.int32, out_ref.shape, 1)
    here = lane // own.shape[1] == which[0]
    out_ref[...] = jnp.where(here, jnp.concatenate([own] * repeats, axis=1), 0.0) - prior


def pack_kernel(mine_ref, other_ref, x_ref, pair_ref, payload_ref):
    samples, dim = mine_ref.shape[0], x_ref.shape[0]
    payload_ref[:samples, :] = mine_ref[...] + other_ref[...]
    payload_ref[samples : samples + dim, :] = x_ref[...]
    payload_ref[samples + dim :, :] = pair_ref[...]


def cand_kernel(which, x_ref, omega_ref, phase_ref, mine_ref, other_ref, out_ref):
    half = mine_ref.shape[1]
    total = omega_ref.shape[1]
    here = pl.multiple_of(which[0] * half, 128)
    there = pl.multiple_of((1 - which[0]) * half, 128)
    out = None
    for start, weights in ((here, mine_ref), (there, other_ref)):
        feats = feature_tile(x_ref[...], omega_ref[:, pl.ds(start, half)], phase_ref[:, pl.ds(start, half)], total)
        part = lax.dot_general(feats, weights[...], (((1,), (1,)), ((), ())), preferred_element_type=f32)
        out = part if out is None else out + part
    out_ref[...] = out


def halves_of(points):
    return three((-0.5 * LOG2E) * jnp.sum(points * points, axis=0, keepdims=True))


def left_of(points):
    stack = left_stack(points * LOG2E, eight_rows(halves_of(points) + [1.0] * 3, points.shape[1]))
    return stack.astype(f32).T.astype(bf16)


def right_of(points):
    return right_stack(points, eight_rows([1.0] * 3 + halves_of(points), points.shape[1]))


def fill(out_ref, left_ref, right_ref):
    rows, columns = out_ref.shape
    for i in range(0, rows, TILE):
        for j in range(0, columns, TILE):
            height, width = min(TILE, rows - i), min(TILE, columns - j)
            exponent = jnp.dot(
                left_ref[i : i + height, :], right_ref[:, j : j + width], preferred_element_type=f32
            )
            out_ref[i : i + height, j : j + width] = jnp.exp2(exponent).astype(bf16)


def points_of(block_ref, samples):
    dim = (block_ref.shape[1] - samples) // 2
    return jnp.concatenate(
        [block_ref[k, samples : samples + dim, :] for k in range(block_ref.shape[0])]
        + [block_ref[k, samples + dim :, :] for k in range(block_ref.shape[0])],
        axis=1,
    )


def rows_of(block_ref, samples, first=0, last=None):
    last = block_ref.shape[0] if last is None else last
    return jnp.concatenate([block_ref[k, :samples, :] for k in range(first, last)], axis=1)


def product(rows, kernel):
    return jnp.dot(rows, kernel, preferred_element_type=f32)


def product_transposed(rows, kernel):
    return lax.dot_general(rows, kernel, (((1,), (1,)), ((), ())), preferred_element_type=f32)


def near_kernel(
    block_ref, cand_ref, left_ref, right_ref, cand_left_ref, kernel_ref, tile_ref, field_ref
):
    samples = field_ref.shape[0]
    points = points_of(block_ref, samples)
    left_ref[...] = left_of(points)
    right_ref[...] = right_of(points)
    cand_left_ref[...] = left_of(cand_ref[...])
    fill(kernel_ref, left_ref, right_ref)
    fill(tile_ref, cand_left_ref, right_ref)
    half = points.shape[1] // 2
    field_ref[...] = product(rows_of(block_ref, samples).astype(bf16), kernel_ref[:half, :])


def far_kernel(
    block_ref, near_ref, left_ref, right_ref, cand_left_ref, before_ref,
    near_far_ref, far_far_ref, tile_ref, field_ref,
    far_left_ref, far_right_ref,
):
    samples = field_ref.shape[0]
    points = points_of(block_ref, samples)
    far_left_ref[...] = left_of(points)
    far_right_ref[...] = right_of(points)
    fill(near_far_ref, left_ref, far_right_ref)
    fill(far_far_ref, far_left_ref, far_right_ref)
    fill(tile_ref, cand_left_ref, far_right_ref)
    half, count = points.shape[1] // 2, points.shape[1]
    near, far = rows_of(near_ref, samples).astype(bf16), rows_of(block_ref, samples).astype(bf16)
    field_ref[:, :count] = before_ref[...] + product_transposed(far, near_far_ref[:, :half])
    field_ref[:, count:] = product(near, near_far_ref[:half, :]) + product(far, far_far_ref[:half, :])


def solve_kernel(
    own_rows, which, near_ref, far_ref, other_ref, before_ref,
    near_near_ref, near_far_ref, far_far_ref,
    near_tile_ref, far_tile_ref, prior_ref, samples_ref, solution_ref,
    image_ref, start_ref, direction_ref, packed_ref,
):
    samples = prior_ref.shape[1]
    blocks, _, width = near_ref.shape
    half = blocks * width
    count = 2 * half
    tiles = [(j, slice(j, j + TILE), slice(j % count, j % count + TILE)) for j in range(0, 2 * count, TILE)]
    for offset, block_ref, first in (
        (0, near_ref, 0), (half, other_ref, 0), (count, far_ref, 0), (count + half, other_ref, blocks)
    ):
        for k in range(blocks):
            start_ref[:, offset + k * width : offset + (k + 1) * width] = block_ref[first + k, :samples, :]
    near = start_ref[:, half:count].astype(bf16)
    far = start_ref[:, count + half :].astype(bf16)

    def total(values):
        return jnp.sum(values, axis=1, keepdims=True)

    zero = jnp.zeros((samples, TILE), f32)
    norm0, curve0, norm1, curve1 = zero, zero, zero, zero
    for j, columns, inner in tiles:
        value = before_ref[:, columns]
        if j < count:
            value += product(near, near_near_ref[half:, inner])
            value += product_transposed(far, near_far_ref[inner, half:])
        else:
            value += product(near, near_far_ref[half:, inner])
            value += product(far, far_far_ref[half:, inner])
        start = start_ref[:, columns]
        image = value + noise_level * start
        image_ref[:, columns] = image
        norm0 += start * start
        curve0 += start * image
    norm0 = total(norm0)
    alpha0 = norm0 / total(curve0)
    for _, columns, _ in tiles:
        residual = start_ref[:, columns] - alpha0 * image_ref[:, columns]
        direction_ref[:, columns] = residual
        norm1 += residual * residual
    norm1 = total(norm1)
    beta = norm1 / norm0
    for _, columns, _ in tiles:
        direction = direction_ref[:, columns] + beta * start_ref[:, columns]
        direction_ref[:, columns] = direction
        packed_ref[:, columns] = direction.astype(bf16)

    for j, columns, inner in tiles:
        diagonal, above = (near_near_ref, None) if j < count else (far_far_ref, near_far_ref)
        value = product(packed_ref[:, columns], diagonal[inner, inner])
        if above is not None:
            value += 2.0 * product(packed_ref[:, :count], above[:, inner])
        if inner.start:
            value += 2.0 * product(packed_ref[:, j - inner.start : j], diagonal[: inner.start, inner])
        direction = direction_ref[:, columns]
        curve1 += direction * (value + noise_level * direction)
    alpha1 = norm1 / total(curve1)
    own = (alpha0 * start_ref[:, :width] + alpha1 * direction_ref[:, :width]).T
    solution_ref[...] = jnp.where(which[0] == 0, own[:own_rows], own[own_rows:])
    value = prior_ref[...]
    for j, columns, inner in tiles:
        weights = (alpha0 * start_ref[:, columns] + alpha1 * direction_ref[:, columns]).astype(bf16)
        tile_ref = near_tile_ref if j < count else far_tile_ref
        value += product_transposed(tile_ref[:, inner], weights)
    samples_ref[...] = value


def call(kernel, out_shape, inputs, scratch=(), scalars=0, hbm=False, flops=0):
    vmem = pl.BlockSpec(memory_space=pltpu.VMEM)
    smem = pl.BlockSpec(memory_space=pltpu.SMEM)
    source = pl.BlockSpec(memory_space=pltpu.HBM) if hbm else vmem
    return pl.pallas_call(
        kernel,
        out_shape=out_shape,
        in_specs=[smem] * scalars + [source] * inputs,
        out_specs=jax.tree.map(lambda _: vmem, out_shape),
        scratch_shapes=list(scratch),
        cost_estimate=pl.CostEstimate(flops=flops, transcendentals=0, bytes_accessed=1 << 20),
        compiler_params=pltpu.CompilerParams(vmem_limit_bytes=16 << 20),
    )


def local_body(x_train, x_cand, targets, noise, omega, phase, prior_weights):
    own_rows, samples = noise.shape
    dim, width = x_train.shape
    blocks = lax.axis_size("train")
    cand_index = lax.axis_index("cand")
    train_index = lax.axis_index("train")
    which = cand_index.astype(jnp.int32).reshape(1)
    phase = phase.reshape(1, -1)
    weights = prior_weights.T
    half_features = weights.shape[1]
    shape = jax.ShapeDtypeStruct
    swap = [(0, 1), (1, 0)]

    def in_hbm(values):
        return pltpu.with_memory_space_constraint(values, pltpu.HBM)

    def exchange(values, bit):
        return lax.ppermute(values, "train", [(i, i ^ bit) for i in range(blocks)])

    pair = exchange(x_train, 1)
    partial = call(
        prior_kernel,
        shape((samples, width), f32),
        scalars=1, inputs=6, hbm=True, flops=1 << 30,
        scratch=[
            pltpu.VMEM((dim, width), f32),
            pltpu.VMEM((dim, half_features), f32),
            pltpu.VMEM((1, half_features), f32),
            pltpu.VMEM(weights.shape, bf16),
            pltpu.VMEM((1, own_rows), f32),
            pltpu.VMEM(noise.shape, f32),
            pltpu.SemaphoreType.DMA((6,)),
        ],
    )(which, *map(in_hbm, (x_train, omega, phase, weights, targets.reshape(1, -1), noise)))
    other = lax.ppermute(partial, "cand", swap)
    payload = call(pack_kernel, shape((samples + 2 * dim, width), f32), inputs=4)(
        partial, other, x_train, pair
    )
    other_weights = lax.ppermute(weights, "cand", swap)
    first = payload[None]
    bit = blocks // 2
    while bit > 4:
        moved = exchange(first, bit)
        first = jnp.concatenate([first, moved], axis=0)
        bit //= 2
    third = exchange(first, 6)
    second = exchange(first, 4)
    near = jnp.concatenate([first, exchange(first, 2)], axis=0)
    far = jnp.concatenate([second, third], axis=0)
    per_device = x_cand.shape[1] // blocks
    mine = lax.dynamic_slice_in_dim(x_cand, train_index * per_device, per_device, 1)
    prior_cand = call(cand_kernel, shape((per_device, samples), f32), scalars=1, inputs=5, flops=1 << 30)(
        which, mine, omega, phase, weights, other_weights
    )
    count = blocks * width // 2
    stack = 6 * dim + 16
    square = shape((count, count), bf16)
    left, right, cand_left, near_near, near_tile, before = call(
        near_kernel,
        (
            shape((count, stack), bf16),
            shape((stack, count), bf16),
            shape((per_device, stack), bf16),
            square,
            shape((per_device, count), bf16),
            shape((samples, count), f32),
        ),
        inputs=2, flops=1 << 31,
    )(near, mine)
    other = exchange(jnp.concatenate([near[:, :samples], far[:, :samples]], axis=0), 1)
    near_far, far_far, far_tile, before = call(
        far_kernel,
        (square, square, shape((per_device, count), bf16), shape((samples, 2 * count), f32)),
        scratch=[pltpu.VMEM((count, stack), bf16), pltpu.VMEM((stack, count), bf16)],
        inputs=6, flops=1 << 33,
    )(far, near, left, right, cand_left, before)
    return tuple(
        call(
            functools.partial(solve_kernel, own_rows),
            (shape((per_device, samples), f32), shape((own_rows, samples), f32)),
            scratch=[
                pltpu.VMEM((samples, 2 * count), f32),
                pltpu.VMEM((samples, 2 * count), f32),
                pltpu.VMEM((samples, 2 * count), f32),
                pltpu.VMEM((samples, 2 * count), bf16),
            ],
            scalars=1, inputs=10, flops=1 << 33,
        )(
            which, near, far, other, before, near_near, near_far, far_far,
            near_tile, far_tile, prior_cand,
        )
    )


def is_local(mesh, x_train):
    train, cand = mesh.shape["train"], mesh.shape["cand"]
    count = x_train.shape[1]
    tiles = count // 2 % TILE == 0
    return cand == 2 and train >= 8 and train & (train - 1) == 0 and tiles and 2 * count * count <= KERNEL_BYTES


def squares_of(points):
    return jnp.sum(points * points, axis=0)


def kernel_tile(row_points, row_norms, column_points, column_norms):
    inner = jnp.dot(row_points.T, column_points, precision=lax.Precision.HIGHEST)
    return jnp.exp(-0.5 * (row_norms[:, None] + column_norms[None, :] - 2.0 * inner)).astype(
        jnp.bfloat16
    )


def features(points, omega, phase):
    angles = jnp.dot(points.T, omega, precision=lax.Precision.HIGHEST) + phase[None, :]
    return (math.sqrt(2.0 / omega.shape[1]) * jnp.cos(angles)).astype(jnp.bfloat16)


def kernel_rows(points, every_point, every_norm, weights):
    count = points.shape[1]
    size = math.gcd(count, 1024)
    stacked = points.reshape(points.shape[0], count // size, size).transpose(1, 0, 2)

    def one_block(block_points):
        tile = kernel_tile(block_points, squares_of(block_points), every_point, every_norm)
        return jnp.dot(tile, weights, preferred_element_type=jnp.float32)

    return lax.map(one_block, stacked).reshape(count, weights.shape[1])


def body(x_train, x_cand, targets, noise, omega, phase, prior_weights):
    own_rows = noise.shape[0]
    cand_index = lax.axis_index("cand")
    train_index = lax.axis_index("train")
    own_points = lax.dynamic_slice_in_dim(x_train, cand_index * own_rows, own_rows, 1)
    full_weights = lax.all_gather(prior_weights, "cand", axis=0, tiled=True)
    prior_train = jnp.dot(
        features(own_points, omega, phase), full_weights, preferred_element_type=jnp.float32
    )
    rhs = targets[:, None] - prior_train - noise
    column_points = lax.all_gather(own_points, "train", axis=1, tiled=True)
    row_norms = squares_of(x_train)
    column_norms = squares_of(column_points)
    width = max(128, 262144 // x_train.shape[1])

    def squares(values):
        return lax.psum(jnp.sum(values * values, axis=0), ("train", "cand"))

    solution = jnp.zeros(rhs.shape, jnp.float32)
    residual = rhs
    direction = rhs
    norm_now = squares(residual)
    for _ in range(ITERS):
        packed = direction.astype(jnp.bfloat16)
        empty = jnp.zeros((x_train.shape[1], packed.shape[1]), jnp.float32)
        total = empty
        piece = lax.all_gather(packed, "train", axis=0, tiled=True)
        for offset in range(0, piece.shape[0], width):
            count = min(width, piece.shape[0] - offset)
            accumulate_points = lax.dynamic_slice_in_dim(column_points, offset, count, 1)
            norms = lax.dynamic_slice_in_dim(column_norms, offset, count, 0)
            tile = kernel_tile(x_train, row_norms, accumulate_points, norms)
            total = total + jnp.dot(
                tile, piece[offset : offset + count], preferred_element_type=jnp.float32
            )
        apply_total = total
        apply_total = lax.psum_scatter(apply_total, "cand", scatter_dimension=0, tiled=True)
        image = apply_total + noise_level * direction
        curve = lax.psum(jnp.sum(direction * image, axis=0), ("train", "cand"))
        alpha = norm_now / curve
        solution = solution + alpha * direction
        residual = residual - alpha * image
        norm_next = squares(residual)
        direction = residual + norm_next / norm_now * direction
        norm_now = norm_next
    per_device = x_cand.shape[1] // lax.axis_size("train")
    mine = lax.dynamic_slice_in_dim(x_cand, train_index * per_device, per_device, 1)
    packed_solution = solution.astype(jnp.bfloat16)
    block_weights = lax.all_gather(packed_solution, "cand", axis=0, tiled=True)
    train_norms = squares_of(x_train)
    kernel_part = lax.psum_scatter(
        kernel_rows(x_cand, x_train, train_norms, block_weights),
        "train",
        scatter_dimension=0,
        tiled=True,
    )
    prior_cand = jnp.dot(
        features(mine, omega, phase), full_weights, preferred_element_type=jnp.float32
    )
    return (prior_cand + kernel_part, solution)


def solution(mesh):
    placed = (
        P(None, "train"),
        P(None, "cand"),
        P(("train", "cand")),
        P(("train", "cand"), None),
        P(),
        P(),
        P("cand", None),
    )

    def sharded(chosen):
        return jax.shard_map(
            chosen,
            mesh=mesh,
            in_specs=placed,
            out_specs=(P(("cand", "train"), None), P(("train", "cand"), None)),
            check_vma=False,
        )

    def step(x_train, *rest):
        if not is_local(mesh, x_train):
            return sharded(body)(x_train, *rest)
        return sharded(local_body)(x_train, *rest)

    return step
```

```python
import functools
import math

import jax
import jax.numpy as jnp
from jax import lax
from jax.experimental import pallas as pl
from jax.experimental.pallas import tpu as pltpu
from jax.sharding import PartitionSpec as P

ITERS = 2


noise_level = 0.5
LOG2E = math.log2(math.e)
COS = (
    1.0,
    -19.739204466576105,
    64.93911592834385,
    -85.4501134274465,
    60.16742979141158,
    -25.96688461044869,
    6.527705959852582,
)
KERNEL_BYTES = 16 << 20
TILE = 256
f32, bf16 = jnp.float32, jnp.bfloat16


def split3(values):
    high = values.astype(bf16)
    rest = values - high.astype(f32)
    middle = rest.astype(bf16)
    low = (rest - middle.astype(f32)).astype(bf16)
    return high, middle, low


def left_stack(values, extra):
    h, m, l = (part.astype(f32) for part in split3(values))
    return jnp.concatenate([h, h, m, m, h, l] + extra, axis=0).astype(bf16)


def right_stack(values, extra):
    h, m, l = (part.astype(f32) for part in split3(values))
    return jnp.concatenate([h, m, h, m, l, h] + extra, axis=0).astype(bf16)


def eight_rows(rows, columns):
    index = lax.broadcasted_iota(jnp.int32, (8, columns), 0)
    out = jnp.zeros((8, columns), f32)
    for k, row in enumerate(rows):
        out = jnp.where(index == k, row, out)
    return [out, jnp.zeros((8, columns), f32)]


def three(values):
    return [part.astype(f32) for part in split3(values)]


def feature_tile(points, omega, phase, total):
    turn = 1.0 / (2.0 * math.pi)
    ones = [1.0] * 3
    left = left_stack(points, eight_rows(ones, points.shape[1]))
    right = right_stack(omega * turn, eight_rows(three(phase * turn), omega.shape[1]))
    turns = lax.dot_general(
        left.astype(f32).T.astype(bf16), right, (((1,), (0,)), ((), ())), preferred_element_type=f32
    )
    rest = turns - jnp.round(turns)
    square = rest * rest
    scale = math.sqrt(2.0 / total)
    value = jnp.full(square.shape, COS[-1] * scale, f32)
    for coefficient in COS[-2::-1]:
        value = value * square + coefficient * scale
    return value.astype(bf16)


def prior_kernel(
    which, x_hbm, omega_hbm, phase_hbm, weights_hbm, targets_hbm, noise_hbm, out_ref,
    x_ref, omega_ref, phase_ref, weights_ref, targets_ref, noise_ref, arrived,
):
    half = weights_hbm.shape[1]
    columns = pl.ds(pl.multiple_of(which[0] * half, 128), half)
    copies = [
        pltpu.make_async_copy(source, target, arrived.at[k])
        for k, (source, target) in enumerate((
            (x_hbm, x_ref),
            (omega_hbm.at[:, columns], omega_ref),
            (phase_hbm.at[:, columns], phase_ref),
            (weights_hbm, weights_ref),
            (targets_hbm, targets_ref),
            (noise_hbm, noise_ref),
        ))
    ]
    for copy in copies:
        copy.start()
    for copy in copies[:3]:
        copy.wait()
    feats = feature_tile(x_ref[...], omega_ref[...], phase_ref[...], omega_hbm.shape[1])
    for copy in copies[3:]:
        copy.wait()
    prior = lax.dot_general(weights_ref[...], feats, (((1,), (1,)), ((), ())), preferred_element_type=f32)
    own = targets_ref[...] - noise_ref[...].T
    repeats = out_ref.shape[1] // own.shape[1]
    lane = lax.broadcasted_iota(jnp.int32, out_ref.shape, 1)
    here = lane // own.shape[1] == which[0]
    out_ref[...] = jnp.where(here, jnp.concatenate([own] * repeats, axis=1), 0.0) - prior


def pack_kernel(mine_ref, other_ref, x_ref, pair_ref, payload_ref):
    samples, dim = mine_ref.shape[0], x_ref.shape[0]
    payload_ref[:samples, :] = mine_ref[...] + other_ref[...]
    payload_ref[samples : samples + dim, :] = x_ref[...]
    payload_ref[samples + dim :, :] = pair_ref[...]


def cand_kernel(which, x_ref, omega_ref, phase_ref, mine_ref, other_ref, out_ref):
    half = mine_ref.shape[1]
    total = omega_ref.shape[1]
    here = pl.multiple_of(which[0] * half, 128)
    there = pl.multiple_of((1 - which[0]) * half, 128)
    out = None
    for start, weights in ((here, mine_ref), (there, other_ref)):
        feats = feature_tile(x_ref[...], omega_ref[:, pl.ds(start, half)], phase_ref[:, pl.ds(start, half)], total)
        part = lax.dot_general(feats, weights[...], (((1,), (1,)), ((), ())), preferred_element_type=f32)
        out = part if out is None else out + part
    out_ref[...] = out


def halves_of(points):
    return three((-0.5 * LOG2E) * jnp.sum(points * points, axis=0, keepdims=True))


def left_of(points):
    stack = left_stack(points * LOG2E, eight_rows(halves_of(points) + [1.0] * 3, points.shape[1]))
    return stack.astype(f32).T.astype(bf16)


def right_of(points):
    return right_stack(points, eight_rows([1.0] * 3 + halves_of(points), points.shape[1]))


def fill(out_ref, left_ref, right_ref, transposed_ref=None):
    rows, columns = out_ref.shape
    for i in range(0, rows, TILE):
        for j in range(i if transposed_ref is out_ref else 0, columns, TILE):
            height, width = min(TILE, rows - i), min(TILE, columns - j)
            exponent = jnp.dot(
                left_ref[i : i + height, :], right_ref[:, j : j + width], preferred_element_type=f32
            )
            tile = jnp.exp2(exponent).astype(bf16)
            out_ref[i : i + height, j : j + width] = tile
            if transposed_ref is not None and (transposed_ref is not out_ref or j > i):
                transposed_ref[j : j + width, i : i + height] = tile.T


def points_of(block_ref, samples):
    dim = (block_ref.shape[1] - samples) // 2
    return jnp.concatenate(
        [block_ref[k, samples : samples + dim, :] for k in range(block_ref.shape[0])]
        + [block_ref[k, samples + dim :, :] for k in range(block_ref.shape[0])],
        axis=1,
    )


def rows_of(block_ref, samples, first=0, last=None):
    last = block_ref.shape[0] if last is None else last
    return jnp.concatenate([block_ref[k, :samples, :] for k in range(first, last)], axis=1)


def product(rows, kernel):
    return jnp.dot(rows, kernel, preferred_element_type=f32)


def product_transposed(rows, kernel):
    return lax.dot_general(rows, kernel, (((1,), (1,)), ((), ())), preferred_element_type=f32)


def near_kernel(
    block_ref, cand_ref, left_ref, right_ref, cand_left_ref, kernel_ref, tile_ref, field_ref
):
    samples = field_ref.shape[0]
    points = points_of(block_ref, samples)
    left_ref[...] = left_of(points)
    right_ref[...] = right_of(points)
    cand_left_ref[...] = left_of(cand_ref[...])
    fill(kernel_ref, left_ref, right_ref)
    fill(tile_ref, cand_left_ref, right_ref)
    half = points.shape[1] // 2
    field_ref[...] = product(rows_of(block_ref, samples).astype(bf16), kernel_ref[:half, :])


def far_kernel(
    block_ref, near_ref, left_ref, right_ref, cand_left_ref, before_ref,
    near_far_ref, far_near_ref, far_far_ref, tile_ref, field_ref,
    far_left_ref, far_right_ref,
):
    samples = field_ref.shape[0]
    points = points_of(block_ref, samples)
    far_left_ref[...] = left_of(points)
    far_right_ref[...] = right_of(points)
    fill(near_far_ref, left_ref, far_right_ref, far_near_ref)
    fill(far_far_ref, far_left_ref, far_right_ref, far_far_ref)
    fill(tile_ref, cand_left_ref, far_right_ref)
    half, count = points.shape[1] // 2, points.shape[1]
    near, far = rows_of(near_ref, samples).astype(bf16), rows_of(block_ref, samples).astype(bf16)
    field_ref[:, :count] = before_ref[...] + product(far, far_near_ref[:half, :])
    field_ref[:, count:] = product(near, near_far_ref[:half, :]) + product(far, far_far_ref[:half, :])


def near_join_kernel(other_ref, before_ref, kernel_ref, field_ref):
    half = kernel_ref.shape[0] // 2
    rows = rows_of(other_ref, other_ref.shape[1]).astype(bf16)
    field_ref[...] = before_ref[...] + product(rows, kernel_ref[half:, :])


def solve_kernel(
    own_rows, which, near_ref, far_ref, near_other_ref, far_other_ref, before_ref,
    near_near_ref, near_far_ref, far_near_ref, far_far_ref,
    near_tile_ref, far_tile_ref, prior_ref, samples_ref, solution_ref,
    image_ref, start_ref, direction_ref, packed_ref,
):
    samples = prior_ref.shape[1]
    blocks, _, width = near_ref.shape
    half = blocks * width
    count = 2 * half
    tiles = [(j, slice(j, j + TILE), slice(j % count, j % count + TILE)) for j in range(0, 2 * count, TILE)]
    for quarter, block_ref in enumerate((near_ref, near_other_ref, far_ref, far_other_ref)):
        for k in range(blocks):
            offset = quarter * half + k * width
            start_ref[:, offset : offset + width] = block_ref[k, :samples, :]
    near = start_ref[:, half:count].astype(bf16)
    far = start_ref[:, count + half :].astype(bf16)

    def total(values):
        return jnp.sum(values, axis=1, keepdims=True)

    zero = jnp.zeros((samples, TILE), f32)
    norm0, curve0, norm1, curve1 = zero, zero, zero, zero
    for j, columns, inner in tiles:
        value = before_ref[:, columns]
        if j < count:
            value += product(far, far_near_ref[half:, inner])
        else:
            value += product(near, near_far_ref[half:, inner])
            value += product(far, far_far_ref[half:, inner])
        start = start_ref[:, columns]
        image = value + noise_level * start
        image_ref[:, columns] = image
        norm0 += start * start
        curve0 += start * image
    norm0 = total(norm0)
    alpha0 = norm0 / total(curve0)
    for _, columns, _ in tiles:
        residual = start_ref[:, columns] - alpha0 * image_ref[:, columns]
        direction_ref[:, columns] = residual
        norm1 += residual * residual
    norm1 = total(norm1)
    beta = norm1 / norm0
    for _, columns, _ in tiles:
        direction = direction_ref[:, columns] + beta * start_ref[:, columns]
        direction_ref[:, columns] = direction
        packed_ref[:, columns] = direction.astype(bf16)

    for j, columns, inner in tiles:
        diagonal, above = (near_near_ref, None) if j < count else (far_far_ref, near_far_ref)
        value = product(packed_ref[:, columns], diagonal[inner, inner])
        if above is not None:
            value += 2.0 * product(packed_ref[:, :count], above[:, inner])
        if inner.start:
            value += 2.0 * product(packed_ref[:, j - inner.start : j], diagonal[: inner.start, inner])
        direction = direction_ref[:, columns]
        curve1 += direction * (value + noise_level * direction)
    alpha1 = norm1 / total(curve1)
    own = (alpha0 * start_ref[:, :width] + alpha1 * direction_ref[:, :width]).T
    solution_ref[...] = jnp.where(which[0] == 0, own[:own_rows], own[own_rows:])
    value = prior_ref[...]
    for j, columns, inner in tiles:
        weights = (alpha0 * start_ref[:, columns] + alpha1 * direction_ref[:, columns]).astype(bf16)
        tile_ref = near_tile_ref if j < count else far_tile_ref
        value += product_transposed(tile_ref[:, inner], weights)
    samples_ref[...] = value


def call(kernel, out_shape, inputs, scratch=(), scalars=0, hbm=False, flops=0):
    vmem = pl.BlockSpec(memory_space=pltpu.VMEM)
    smem = pl.BlockSpec(memory_space=pltpu.SMEM)
    source = pl.BlockSpec(memory_space=pltpu.HBM) if hbm else vmem
    return pl.pallas_call(
        kernel,
        out_shape=out_shape,
        in_specs=[smem] * scalars + [source] * inputs,
        out_specs=jax.tree.map(lambda _: vmem, out_shape),
        scratch_shapes=list(scratch),
        cost_estimate=pl.CostEstimate(flops=flops, transcendentals=0, bytes_accessed=1 << 20),
        compiler_params=pltpu.CompilerParams(vmem_limit_bytes=16 << 20),
    )


def local_body(x_train, x_cand, targets, noise, omega, phase, prior_weights):
    own_rows, samples = noise.shape
    dim, width = x_train.shape
    blocks = lax.axis_size("train")
    cand_index = lax.axis_index("cand")
    train_index = lax.axis_index("train")
    which = cand_index.astype(jnp.int32).reshape(1)
    phase = phase.reshape(1, -1)
    weights = prior_weights.T
    half_features = weights.shape[1]
    shape = jax.ShapeDtypeStruct
    swap = [(0, 1), (1, 0)]

    def in_hbm(values):
        return pltpu.with_memory_space_constraint(values, pltpu.HBM)

    def exchange(values, bit):
        return lax.ppermute(values, "train", [(i, i ^ bit) for i in range(blocks)])

    pair = exchange(x_train, 1)
    partial = call(
        prior_kernel,
        shape((samples, width), f32),
        scalars=1, inputs=6, hbm=True, flops=1 << 30,
        scratch=[
            pltpu.VMEM((dim, width), f32),
            pltpu.VMEM((dim, half_features), f32),
            pltpu.VMEM((1, half_features), f32),
            pltpu.VMEM(weights.shape, bf16),
            pltpu.VMEM((1, own_rows), f32),
            pltpu.VMEM(noise.shape, f32),
            pltpu.SemaphoreType.DMA((6,)),
        ],
    )(which, *map(in_hbm, (x_train, omega, phase, weights, targets.reshape(1, -1), noise)))
    other = lax.ppermute(partial, "cand", swap)
    payload = call(pack_kernel, shape((samples + 2 * dim, width), f32), inputs=4)(
        partial, other, x_train, pair
    )
    other_weights = lax.ppermute(weights, "cand", swap)
    first = payload[None]
    bit = blocks // 2
    while bit > 4:
        moved = exchange(first, bit)
        first = jnp.concatenate([first, moved], axis=0)
        bit //= 2
    third = exchange(first, 6)
    second = exchange(first, 4)
    near = jnp.concatenate([first, exchange(first, 2)], axis=0)
    far = jnp.concatenate([second, third], axis=0)
    per_device = x_cand.shape[1] // blocks
    mine = lax.dynamic_slice_in_dim(x_cand, train_index * per_device, per_device, 1)
    prior_cand = call(cand_kernel, shape((per_device, samples), f32), scalars=1, inputs=5, flops=1 << 30)(
        which, mine, omega, phase, weights, other_weights
    )
    count = blocks * width // 2
    stack = 6 * dim + 16
    square = shape((count, count), bf16)
    left, right, cand_left, near_near, near_tile, before = call(
        near_kernel,
        (
            shape((count, stack), bf16),
            shape((stack, count), bf16),
            shape((per_device, stack), bf16),
            square,
            shape((per_device, count), bf16),
            shape((samples, count), f32),
        ),
        inputs=2, flops=1 << 31,
    )(near, mine)
    near_other = exchange(near[:, :samples], 1)
    before = call(near_join_kernel, shape((samples, count), f32), inputs=3, flops=1 << 30)(
        near_other, before, near_near
    )
    far_other = exchange(far[:, :samples], 1)
    near_far, far_near, far_far, far_tile, before = call(
        far_kernel,
        (square, square, square, shape((per_device, count), bf16), shape((samples, 2 * count), f32)),
        scratch=[pltpu.VMEM((count, stack), bf16), pltpu.VMEM((stack, count), bf16)],
        inputs=6, flops=1 << 33,
    )(far, near, left, right, cand_left, before)
    return tuple(
        call(
            functools.partial(solve_kernel, own_rows),
            (shape((per_device, samples), f32), shape((own_rows, samples), f32)),
            scratch=[
                pltpu.VMEM((samples, 2 * count), f32),
                pltpu.VMEM((samples, 2 * count), f32),
                pltpu.VMEM((samples, 2 * count), f32),
                pltpu.VMEM((samples, 2 * count), bf16),
            ],
            scalars=1, inputs=12, flops=1 << 33,
        )(
            which, near, far, near_other, far_other, before, near_near, near_far, far_near, far_far,
            near_tile, far_tile, prior_cand,
        )
    )


def is_local(mesh, x_train):
    train, cand = mesh.shape["train"], mesh.shape["cand"]
    count = x_train.shape[1]
    tiles = count // 2 % TILE == 0
    return cand == 2 and train >= 8 and train & (train - 1) == 0 and tiles and 2 * count * count <= KERNEL_BYTES


def squares_of(points):
    return jnp.sum(points * points, axis=0)


def kernel_tile(row_points, row_norms, column_points, column_norms):
    inner = jnp.dot(row_points.T, column_points, precision=lax.Precision.HIGHEST)
    return jnp.exp(-0.5 * (row_norms[:, None] + column_norms[None, :] - 2.0 * inner)).astype(
        jnp.bfloat16
    )


def features(points, omega, phase):
    angles = jnp.dot(points.T, omega, precision=lax.Precision.HIGHEST) + phase[None, :]
    return (math.sqrt(2.0 / omega.shape[1]) * jnp.cos(angles)).astype(jnp.bfloat16)


def kernel_rows(points, every_point, every_norm, weights):
    count = points.shape[1]
    size = math.gcd(count, 1024)
    stacked = points.reshape(points.shape[0], count // size, size).transpose(1, 0, 2)

    def one_block(block_points):
        tile = kernel_tile(block_points, squares_of(block_points), every_point, every_norm)
        return jnp.dot(tile, weights, preferred_element_type=jnp.float32)

    return lax.map(one_block, stacked).reshape(count, weights.shape[1])


def body(x_train, x_cand, targets, noise, omega, phase, prior_weights):
    own_rows = noise.shape[0]
    cand_index = lax.axis_index("cand")
    train_index = lax.axis_index("train")
    own_points = lax.dynamic_slice_in_dim(x_train, cand_index * own_rows, own_rows, 1)
    full_weights = lax.all_gather(prior_weights, "cand", axis=0, tiled=True)
    prior_train = jnp.dot(
        features(own_points, omega, phase), full_weights, preferred_element_type=jnp.float32
    )
    rhs = targets[:, None] - prior_train - noise
    column_points = lax.all_gather(own_points, "train", axis=1, tiled=True)
    row_norms = squares_of(x_train)
    column_norms = squares_of(column_points)
    width = max(128, 262144 // x_train.shape[1])

    def squares(values):
        return lax.psum(jnp.sum(values * values, axis=0), ("train", "cand"))

    solution = jnp.zeros(rhs.shape, jnp.float32)
    residual = rhs
    direction = rhs
    norm_now = squares(residual)
    for _ in range(ITERS):
        packed = direction.astype(jnp.bfloat16)
        empty = jnp.zeros((x_train.shape[1], packed.shape[1]), jnp.float32)
        total = empty
        piece = lax.all_gather(packed, "train", axis=0, tiled=True)
        for offset in range(0, piece.shape[0], width):
            count = min(width, piece.shape[0] - offset)
            accumulate_points = lax.dynamic_slice_in_dim(column_points, offset, count, 1)
            norms = lax.dynamic_slice_in_dim(column_norms, offset, count, 0)
            tile = kernel_tile(x_train, row_norms, accumulate_points, norms)
            total = total + jnp.dot(
                tile, piece[offset : offset + count], preferred_element_type=jnp.float32
            )
        apply_total = total
        apply_total = lax.psum_scatter(apply_total, "cand", scatter_dimension=0, tiled=True)
        image = apply_total + noise_level * direction
        curve = lax.psum(jnp.sum(direction * image, axis=0), ("train", "cand"))
        alpha = norm_now / curve
        solution = solution + alpha * direction
        residual = residual - alpha * image
        norm_next = squares(residual)
        direction = residual + norm_next / norm_now * direction
        norm_now = norm_next
    per_device = x_cand.shape[1] // lax.axis_size("train")
    mine = lax.dynamic_slice_in_dim(x_cand, train_index * per_device, per_device, 1)
    packed_solution = solution.astype(jnp.bfloat16)
    block_weights = lax.all_gather(packed_solution, "cand", axis=0, tiled=True)
    train_norms = squares_of(x_train)
    kernel_part = lax.psum_scatter(
        kernel_rows(x_cand, x_train, train_norms, block_weights),
        "train",
        scatter_dimension=0,
        tiled=True,
    )
    prior_cand = jnp.dot(
        features(mine, omega, phase), full_weights, preferred_element_type=jnp.float32
    )
    return (prior_cand + kernel_part, solution)


def solution(mesh):
    placed = (
        P(None, "train"),
        P(None, "cand"),
        P(("train", "cand")),
        P(("train", "cand"), None),
        P(),
        P(),
        P("cand", None),
    )

    def sharded(chosen):
        return jax.shard_map(
            chosen,
            mesh=mesh,
            in_specs=placed,
            out_specs=(P(("cand", "train"), None), P(("train", "cand"), None)),
            check_vma=False,
        )

    def step(x_train, *rest):
        if not is_local(mesh, x_train):
            return sharded(body)(x_train, *rest)
        return sharded(local_body)(x_train, *rest)

    return step
```

```python
import functools
import math

import jax
import jax.numpy as jnp
from jax import lax
from jax.experimental import pallas as pl
from jax.experimental.pallas import tpu as pltpu
from jax.sharding import PartitionSpec as P

ITERS = 2


noise_level = 0.5
LOG2E = math.log2(math.e)
COS = (
    1.0,
    -19.739204466576105,
    64.93911592834385,
    -85.4501134274465,
    60.16742979141158,
    -25.96688461044869,
    6.527705959852582,
)
KERNEL_BYTES = 16 << 20
TILE = 256
f32, bf16 = jnp.float32, jnp.bfloat16


def split3(values):
    high = values.astype(bf16)
    rest = values - high.astype(f32)
    middle = rest.astype(bf16)
    low = (rest - middle.astype(f32)).astype(bf16)
    return high, middle, low


def left_stack(values, extra):
    h, m, l = (part.astype(f32) for part in split3(values))
    return jnp.concatenate([h, h, m, m, h, l] + extra, axis=0).astype(bf16)


def right_stack(values, extra):
    h, m, l = (part.astype(f32) for part in split3(values))
    return jnp.concatenate([h, m, h, m, l, h] + extra, axis=0).astype(bf16)


def eight_rows(rows, columns):
    index = lax.broadcasted_iota(jnp.int32, (8, columns), 0)
    out = jnp.zeros((8, columns), f32)
    for k, row in enumerate(rows):
        out = jnp.where(index == k, row, out)
    return [out, jnp.zeros((8, columns), f32)]


def three(values):
    return [part.astype(f32) for part in split3(values)]


def feature_tile(points, omega, phase, total):
    turn = 1.0 / (2.0 * math.pi)
    ones = [1.0] * 3
    left = left_stack(points, eight_rows(ones, points.shape[1]))
    right = right_stack(omega * turn, eight_rows(three(phase * turn), omega.shape[1]))
    turns = lax.dot_general(
        left.astype(f32).T.astype(bf16), right, (((1,), (0,)), ((), ())), preferred_element_type=f32
    )
    rest = turns - jnp.round(turns)
    square = rest * rest
    scale = math.sqrt(2.0 / total)
    value = jnp.full(square.shape, COS[-1] * scale, f32)
    for coefficient in COS[-2::-1]:
        value = value * square + coefficient * scale
    return value.astype(bf16)


def prior_kernel(
    which, x_hbm, omega_hbm, phase_hbm, weights_hbm, targets_hbm, noise_hbm, out_ref,
    x_ref, omega_ref, phase_ref, weights_ref, targets_ref, noise_ref, arrived,
):
    half = weights_hbm.shape[1]
    columns = pl.ds(pl.multiple_of(which[0] * half, 128), half)
    copies = [
        pltpu.make_async_copy(source, target, arrived.at[k])
        for k, (source, target) in enumerate((
            (x_hbm, x_ref),
            (omega_hbm.at[:, columns], omega_ref),
            (phase_hbm.at[:, columns], phase_ref),
            (weights_hbm, weights_ref),
            (targets_hbm, targets_ref),
            (noise_hbm, noise_ref),
        ))
    ]
    for copy in copies:
        copy.start()
    for copy in copies[:3]:
        copy.wait()
    feats = feature_tile(x_ref[...], omega_ref[...], phase_ref[...], omega_hbm.shape[1])
    for copy in copies[3:]:
        copy.wait()
    prior = lax.dot_general(weights_ref[...], feats, (((1,), (1,)), ((), ())), preferred_element_type=f32)
    own = targets_ref[...] - noise_ref[...].T
    repeats = out_ref.shape[1] // own.shape[1]
    lane = lax.broadcasted_iota(jnp.int32, out_ref.shape, 1)
    here = lane // own.shape[1] == which[0]
    out_ref[...] = jnp.where(here, jnp.concatenate([own] * repeats, axis=1), 0.0) - prior


def pack_kernel(mine_ref, other_ref, x_ref, pair_ref, payload_ref):
    samples, dim = mine_ref.shape[0], x_ref.shape[0]
    payload_ref[:samples, :] = mine_ref[...] + other_ref[...]
    payload_ref[samples : samples + dim, :] = x_ref[...]
    payload_ref[samples + dim :, :] = pair_ref[...]


def cand_kernel(which, x_ref, omega_ref, phase_ref, mine_ref, other_ref, out_ref):
    half = mine_ref.shape[1]
    total = omega_ref.shape[1]
    here = pl.multiple_of(which[0] * half, 128)
    there = pl.multiple_of((1 - which[0]) * half, 128)
    out = None
    for start, weights in ((here, mine_ref), (there, other_ref)):
        feats = feature_tile(x_ref[...], omega_ref[:, pl.ds(start, half)], phase_ref[:, pl.ds(start, half)], total)
        part = lax.dot_general(feats, weights[...], (((1,), (1,)), ((), ())), preferred_element_type=f32)
        out = part if out is None else out + part
    out_ref[...] = out


def halves_of(points):
    return three((-0.5 * LOG2E) * jnp.sum(points * points, axis=0, keepdims=True))


def left_of(points):
    stack = left_stack(points * LOG2E, eight_rows(halves_of(points) + [1.0] * 3, points.shape[1]))
    return stack.astype(f32).T.astype(bf16)


def right_of(points):
    return right_stack(points, eight_rows([1.0] * 3 + halves_of(points), points.shape[1]))


def fill(out_ref, left_ref, right_ref, transposed_ref=None):
    rows, columns = out_ref.shape
    for i in range(0, rows, TILE):
        for j in range(i if transposed_ref is out_ref else 0, columns, TILE):
            height, width = min(TILE, rows - i), min(TILE, columns - j)
            exponent = jnp.dot(
                left_ref[i : i + height, :], right_ref[:, j : j + width], preferred_element_type=f32
            )
            tile = jnp.exp2(exponent).astype(bf16)
            out_ref[i : i + height, j : j + width] = tile
            if transposed_ref is not None and (transposed_ref is not out_ref or j > i):
                transposed_ref[j : j + width, i : i + height] = tile.T


def points_of(block_ref, samples):
    dim = (block_ref.shape[1] - samples) // 2
    return jnp.concatenate(
        [block_ref[k, samples : samples + dim, :] for k in range(block_ref.shape[0])]
        + [block_ref[k, samples + dim :, :] for k in range(block_ref.shape[0])],
        axis=1,
    )


def rows_of(block_ref, samples, first=0, last=None):
    last = block_ref.shape[0] if last is None else last
    return jnp.concatenate([block_ref[k, :samples, :] for k in range(first, last)], axis=1)


def product(rows, kernel):
    return jnp.dot(rows, kernel, preferred_element_type=f32)


def product_transposed(rows, kernel):
    return lax.dot_general(rows, kernel, (((1,), (1,)), ((), ())), preferred_element_type=f32)


def near_kernel(
    block_ref, cand_ref, left_ref, right_ref, cand_left_ref, kernel_ref, tile_ref, field_ref
):
    samples = field_ref.shape[0]
    points = points_of(block_ref, samples)
    left_ref[...] = left_of(points)
    right_ref[...] = right_of(points)
    cand_left_ref[...] = left_of(cand_ref[...])
    fill(kernel_ref, left_ref, right_ref)
    fill(tile_ref, cand_left_ref, right_ref)
    half = points.shape[1] // 2
    field_ref[...] = product(rows_of(block_ref, samples).astype(bf16), kernel_ref[:half, :])


def side_kernel(
    block_ref, near_ref, left_ref, right_ref, cand_left_ref, before_ref,
    side_left_ref, side_right_ref, near_side_ref, side_near_ref, side_ref, tile_ref, near_field_ref, field_ref,
):
    samples, size = field_ref.shape
    points = points_of(block_ref, samples)
    side_left_ref[...] = left_of(points)
    side_right_ref[...] = right_of(points)
    fill(near_side_ref, left_ref, side_right_ref, side_near_ref)
    fill(side_ref, side_left_ref, side_right_ref, side_ref)
    fill(tile_ref, cand_left_ref, side_right_ref)
    near, side = rows_of(near_ref, samples).astype(bf16), rows_of(block_ref, samples).astype(bf16)
    near_field_ref[...] = before_ref[...] + product(side, side_near_ref[: size // 2, :])
    field_ref[...] = product(near, near_side_ref[: near.shape[1], :]) + product(side, side_ref[: size // 2, :])


def last_kernel(
    block_ref, near_ref, side_block_ref, left_ref, right_ref, cand_left_ref, side_left_ref, side_right_ref,
    near_before_ref, side_before_ref, near_other_ref, near_near_ref,
    near_last_ref, last_near_ref, side_last_ref, last_side_ref, last_ref, tile_ref, field_ref,
    last_left_ref, last_right_ref,
):
    samples = field_ref.shape[0]
    points = points_of(block_ref, samples)
    last_left_ref[...] = left_of(points)
    last_right_ref[...] = right_of(points)
    fill(near_last_ref, left_ref, last_right_ref, last_near_ref)
    fill(side_last_ref, side_left_ref, last_right_ref, last_side_ref)
    fill(last_ref, last_left_ref, last_right_ref, last_ref)
    fill(tile_ref, cand_left_ref, last_right_ref)
    count, size = near_before_ref.shape[1], points.shape[1]
    half = size // 2
    near, side, last = (
        rows_of(ref, samples).astype(bf16) for ref in (near_ref, side_block_ref, block_ref)
    )
    other = rows_of(near_other_ref, samples).astype(bf16)
    field_ref[:, :count] = (
        near_before_ref[...] + product(last, last_near_ref[:half, :]) + product(other, near_near_ref[size:, :])
    )
    field_ref[:, count : count + size] = side_before_ref[...] + product(last, last_side_ref[:half, :])
    field_ref[:, count + size :] = (
        product(near, near_last_ref[: near.shape[1], :])
        + product(side, side_last_ref[:half, :])
        + product(last, last_ref[:half, :])
    )


def solve_kernel(
    own_rows, which, near_ref, side_block_ref, last_block_ref, near_other_ref, far_other_ref, before_ref,
    near_near_ref, near_side_ref, side_near_ref, side_ref,
    near_last_ref, last_near_ref, side_last_ref, last_side_ref, last_ref,
    near_tile_ref, side_tile_ref, last_tile_ref, prior_ref, samples_ref, solution_ref,
    image_ref, start_ref, direction_ref, packed_ref,
):
    samples = prior_ref.shape[1]
    width = near_ref.shape[2]
    count, size = near_side_ref.shape
    half = size // 2
    few = half // width
    position = 0
    for block_ref, first, blocks in (
        (near_ref, 0, 2 * few), (near_other_ref, 0, 2 * few),
        (side_block_ref, 0, few), (far_other_ref, few, few),
        (last_block_ref, 0, few), (far_other_ref, 0, few),
    ):
        for k in range(first, first + blocks):
            start_ref[:, position : position + width] = block_ref[k, :samples, :]
            position += width
    near = start_ref[:, size:count].astype(bf16)
    side = start_ref[:, count + half : count + size].astype(bf16)
    last = start_ref[:, count + size + half :].astype(bf16)
    segments = (
        (0, count, ((side, side_near_ref, half), (last, last_near_ref, half)), (), near_near_ref, near_tile_ref),
        (
            count, size,
            ((near, near_side_ref, size), (side, side_ref, half), (last, last_side_ref, half)),
            ((0, near_side_ref),), side_ref, side_tile_ref,
        ),
        (
            count + size, size,
            ((near, near_last_ref, size), (side, side_last_ref, half), (last, last_ref, half)),
            ((0, near_last_ref), (count, side_last_ref)), last_ref, last_tile_ref,
        ),
    )
    tiles = [
        (slice(offset + j, offset + j + TILE), slice(j, j + TILE), offset, *segment)
        for offset, extent, *segment in segments
        for j in range(0, extent, TILE)
    ]

    def total(values):
        return jnp.sum(values, axis=1, keepdims=True)

    zero = jnp.zeros((samples, TILE), f32)
    norm0, curve0, norm1, curve1 = zero, zero, zero, zero
    for columns, inner, _, products, *_ in tiles:
        value = before_ref[:, columns]
        for rows, kernel_ref, first in products:
            value += product(rows, kernel_ref[first:, inner])
        start = start_ref[:, columns]
        image = value + noise_level * start
        image_ref[:, columns] = image
        norm0 += start * start
        curve0 += start * image
    norm0 = total(norm0)
    alpha0 = norm0 / total(curve0)
    for columns, *_ in tiles:
        residual = start_ref[:, columns] - alpha0 * image_ref[:, columns]
        direction_ref[:, columns] = residual
        norm1 += residual * residual
    norm1 = total(norm1)
    beta = norm1 / norm0
    for columns, *_ in tiles:
        direction = direction_ref[:, columns] + beta * start_ref[:, columns]
        direction_ref[:, columns] = direction
        packed_ref[:, columns] = direction.astype(bf16)

    for columns, inner, offset, _, above, diagonal, _ in tiles:
        value = product(packed_ref[:, columns], diagonal[inner, inner])
        for first, kernel_ref in above:
            rows = packed_ref[:, first : first + kernel_ref.shape[0]]
            value += 2.0 * product(rows, kernel_ref[:, inner])
        if inner.start:
            rows = packed_ref[:, offset : offset + inner.start]
            value += 2.0 * product(rows, diagonal[: inner.start, inner])
        direction = direction_ref[:, columns]
        curve1 += direction * (value + noise_level * direction)
    alpha1 = norm1 / total(curve1)
    own = (alpha0 * start_ref[:, :width] + alpha1 * direction_ref[:, :width]).T
    solution_ref[...] = jnp.where(which[0] == 0, own[:own_rows], own[own_rows:])
    value = prior_ref[...]
    for columns, inner, *_, tile_ref in tiles:
        weights = (alpha0 * start_ref[:, columns] + alpha1 * direction_ref[:, columns]).astype(bf16)
        value += product_transposed(tile_ref[:, inner], weights)
    samples_ref[...] = value


def call(kernel, out_shape, inputs, scratch=(), scalars=0, hbm=False, flops=0):
    vmem = pl.BlockSpec(memory_space=pltpu.VMEM)
    smem = pl.BlockSpec(memory_space=pltpu.SMEM)
    source = pl.BlockSpec(memory_space=pltpu.HBM) if hbm else vmem
    return pl.pallas_call(
        kernel,
        out_shape=out_shape,
        in_specs=[smem] * scalars + [source] * inputs,
        out_specs=jax.tree.map(lambda _: vmem, out_shape),
        scratch_shapes=list(scratch),
        cost_estimate=pl.CostEstimate(flops=flops, transcendentals=0, bytes_accessed=1 << 20),
        compiler_params=pltpu.CompilerParams(vmem_limit_bytes=16 << 20),
    )


def local_body(x_train, x_cand, targets, noise, omega, phase, prior_weights):
    own_rows, samples = noise.shape
    dim, width = x_train.shape
    blocks = lax.axis_size("train")
    cand_index = lax.axis_index("cand")
    train_index = lax.axis_index("train")
    which = cand_index.astype(jnp.int32).reshape(1)
    phase = phase.reshape(1, -1)
    weights = prior_weights.T
    half_features = weights.shape[1]
    shape = jax.ShapeDtypeStruct
    swap = [(0, 1), (1, 0)]

    def in_hbm(values):
        return pltpu.with_memory_space_constraint(values, pltpu.HBM)

    def exchange(values, bit):
        return lax.ppermute(values, "train", [(i, i ^ bit) for i in range(blocks)])

    pair = exchange(x_train, 1)
    partial = call(
        prior_kernel,
        shape((samples, width), f32),
        scalars=1, inputs=6, hbm=True, flops=1 << 30,
        scratch=[
            pltpu.VMEM((dim, width), f32),
            pltpu.VMEM((dim, half_features), f32),
            pltpu.VMEM((1, half_features), f32),
            pltpu.VMEM(weights.shape, bf16),
            pltpu.VMEM((1, own_rows), f32),
            pltpu.VMEM(noise.shape, f32),
            pltpu.SemaphoreType.DMA((6,)),
        ],
    )(which, *map(in_hbm, (x_train, omega, phase, weights, targets.reshape(1, -1), noise)))
    other = lax.ppermute(partial, "cand", swap)
    payload = call(pack_kernel, shape((samples + 2 * dim, width), f32), inputs=4)(
        partial, other, x_train, pair
    )
    other_weights = lax.ppermute(weights, "cand", swap)
    first = payload[None]
    bit = blocks // 2
    while bit > 4:
        moved = exchange(first, bit)
        first = jnp.concatenate([first, moved], axis=0)
        bit //= 2
    third = exchange(first, 6)
    second = exchange(first, 4)
    near = jnp.concatenate([first, exchange(first, 2)], axis=0)
    per_device = x_cand.shape[1] // blocks
    mine = lax.dynamic_slice_in_dim(x_cand, train_index * per_device, per_device, 1)
    prior_cand = call(cand_kernel, shape((per_device, samples), f32), scalars=1, inputs=5, flops=1 << 30)(
        which, mine, omega, phase, weights, other_weights
    )
    count = blocks * width // 2
    stack = 6 * dim + 16
    square = shape((count, count), bf16)
    left, right, cand_left, near_near, near_tile, before = call(
        near_kernel,
        (
            shape((count, stack), bf16),
            shape((stack, count), bf16),
            shape((per_device, stack), bf16),
            square,
            shape((per_device, count), bf16),
            shape((samples, count), f32),
        ),
        inputs=2, flops=1 << 31,
    )(near, mine)
    near_other = exchange(near[:, :samples], 1)
    size = count // 2

    def kernels(*shapes):
        return tuple(shape(dims, bf16) for dims in shapes)

    (side_left, side_right, near_side, side_near, side, side_tile, before, side_before) = call(
        side_kernel,
        kernels((size, stack), (stack, size), (count, size), (size, count), (size, size), (per_device, size))
        + (shape((samples, count), f32), shape((samples, size), f32)),
        inputs=6, flops=1 << 31,
    )(third, near, left, right, cand_left, before)
    far_other = exchange(jnp.concatenate([second[:, :samples], third[:, :samples]], axis=0), 1)
    near_last, last_near, side_last, last_side, last, last_tile, before = call(
        last_kernel,
        kernels((count, size), (size, count), (size, size), (size, size), (size, size), (per_device, size))
        + (shape((samples, 2 * count), f32),),
        scratch=[pltpu.VMEM((size, stack), bf16), pltpu.VMEM((stack, size), bf16)],
        inputs=12, flops=1 << 32,
    )(
        second, near, third, left, right, cand_left, side_left, side_right, before, side_before,
        near_other, near_near,
    )
    return tuple(
        call(
            functools.partial(solve_kernel, own_rows),
            (shape((per_device, samples), f32), shape((own_rows, samples), f32)),
            scratch=[
                pltpu.VMEM((samples, 2 * count), f32),
                pltpu.VMEM((samples, 2 * count), f32),
                pltpu.VMEM((samples, 2 * count), f32),
                pltpu.VMEM((samples, 2 * count), bf16),
            ],
            scalars=1, inputs=19, flops=1 << 33,
        )(
            which, near, third, second, near_other, far_other, before,
            near_near, near_side, side_near, side,
            near_last, last_near, side_last, last_side, last,
            near_tile, side_tile, last_tile, prior_cand,
        )
    )


def is_local(mesh, x_train):
    train, cand = mesh.shape["train"], mesh.shape["cand"]
    count = x_train.shape[1]
    tiles = count // 4 % TILE == 0
    return cand == 2 and train >= 8 and train & (train - 1) == 0 and tiles and 2 * count * count <= KERNEL_BYTES


def squares_of(points):
    return jnp.sum(points * points, axis=0)


def kernel_tile(row_points, row_norms, column_points, column_norms):
    inner = jnp.dot(row_points.T, column_points, precision=lax.Precision.HIGHEST)
    return jnp.exp(-0.5 * (row_norms[:, None] + column_norms[None, :] - 2.0 * inner)).astype(
        jnp.bfloat16
    )


def features(points, omega, phase):
    angles = jnp.dot(points.T, omega, precision=lax.Precision.HIGHEST) + phase[None, :]
    return (math.sqrt(2.0 / omega.shape[1]) * jnp.cos(angles)).astype(jnp.bfloat16)


def kernel_rows(points, every_point, every_norm, weights):
    count = points.shape[1]
    size = math.gcd(count, 1024)
    stacked = points.reshape(points.shape[0], count // size, size).transpose(1, 0, 2)

    def one_block(block_points):
        tile = kernel_tile(block_points, squares_of(block_points), every_point, every_norm)
        return jnp.dot(tile, weights, preferred_element_type=jnp.float32)

    return lax.map(one_block, stacked).reshape(count, weights.shape[1])


def body(x_train, x_cand, targets, noise, omega, phase, prior_weights):
    own_rows = noise.shape[0]
    cand_index = lax.axis_index("cand")
    train_index = lax.axis_index("train")
    own_points = lax.dynamic_slice_in_dim(x_train, cand_index * own_rows, own_rows, 1)
    full_weights = lax.all_gather(prior_weights, "cand", axis=0, tiled=True)
    prior_train = jnp.dot(
        features(own_points, omega, phase), full_weights, preferred_element_type=jnp.float32
    )
    rhs = targets[:, None] - prior_train - noise
    column_points = lax.all_gather(own_points, "train", axis=1, tiled=True)
    row_norms = squares_of(x_train)
    column_norms = squares_of(column_points)
    width = max(128, 262144 // x_train.shape[1])

    def squares(values):
        return lax.psum(jnp.sum(values * values, axis=0), ("train", "cand"))

    solution = jnp.zeros(rhs.shape, jnp.float32)
    residual = rhs
    direction = rhs
    norm_now = squares(residual)
    for _ in range(ITERS):
        packed = direction.astype(jnp.bfloat16)
        empty = jnp.zeros((x_train.shape[1], packed.shape[1]), jnp.float32)
        total = empty
        piece = lax.all_gather(packed, "train", axis=0, tiled=True)
        for offset in range(0, piece.shape[0], width):
            count = min(width, piece.shape[0] - offset)
            accumulate_points = lax.dynamic_slice_in_dim(column_points, offset, count, 1)
            norms = lax.dynamic_slice_in_dim(column_norms, offset, count, 0)
            tile = kernel_tile(x_train, row_norms, accumulate_points, norms)
            total = total + jnp.dot(
                tile, piece[offset : offset + count], preferred_element_type=jnp.float32
            )
        apply_total = total
        apply_total = lax.psum_scatter(apply_total, "cand", scatter_dimension=0, tiled=True)
        image = apply_total + noise_level * direction
        curve = lax.psum(jnp.sum(direction * image, axis=0), ("train", "cand"))
        alpha = norm_now / curve
        solution = solution + alpha * direction
        residual = residual - alpha * image
        norm_next = squares(residual)
        direction = residual + norm_next / norm_now * direction
        norm_now = norm_next
    per_device = x_cand.shape[1] // lax.axis_size("train")
    mine = lax.dynamic_slice_in_dim(x_cand, train_index * per_device, per_device, 1)
    packed_solution = solution.astype(jnp.bfloat16)
    block_weights = lax.all_gather(packed_solution, "cand", axis=0, tiled=True)
    train_norms = squares_of(x_train)
    kernel_part = lax.psum_scatter(
        kernel_rows(x_cand, x_train, train_norms, block_weights),
        "train",
        scatter_dimension=0,
        tiled=True,
    )
    prior_cand = jnp.dot(
        features(mine, omega, phase), full_weights, preferred_element_type=jnp.float32
    )
    return (prior_cand + kernel_part, solution)


def solution(mesh):
    placed = (
        P(None, "train"),
        P(None, "cand"),
        P(("train", "cand")),
        P(("train", "cand"), None),
        P(),
        P(),
        P("cand", None),
    )

    def sharded(chosen):
        return jax.shard_map(
            chosen,
            mesh=mesh,
            in_specs=placed,
            out_specs=(P(("cand", "train"), None), P(("train", "cand"), None)),
            check_vma=False,
        )

    def step(x_train, *rest):
        if not is_local(mesh, x_train):
            return sharded(body)(x_train, *rest)
        return sharded(local_body)(x_train, *rest)

    return step
```

```python
import functools
import math

import jax
import jax.numpy as jnp
from jax import lax
from jax.experimental import pallas as pl
from jax.experimental.pallas import tpu as pltpu
from jax.sharding import PartitionSpec as P

ITERS = 2


noise_level = 0.5
LOG2E = math.log2(math.e)
COS = (
    1.0,
    -19.739204466576105,
    64.93911592834385,
    -85.4501134274465,
    60.16742979141158,
    -25.96688461044869,
    6.527705959852582,
)
KERNEL_BYTES = 16 << 20
TILE = 256
f32, bf16 = jnp.float32, jnp.bfloat16


def split3(values):
    high = values.astype(bf16)
    rest = values - high.astype(f32)
    middle = rest.astype(bf16)
    low = (rest - middle.astype(f32)).astype(bf16)
    return high, middle, low


def left_stack(values, extra):
    h, m, l = (part.astype(f32) for part in split3(values))
    return jnp.concatenate([h, h, m, m, h, l] + extra, axis=0).astype(bf16)


def right_stack(values, extra):
    h, m, l = (part.astype(f32) for part in split3(values))
    return jnp.concatenate([h, m, h, m, l, h] + extra, axis=0).astype(bf16)


def eight_rows(rows, columns):
    index = lax.broadcasted_iota(jnp.int32, (8, columns), 0)
    out = jnp.zeros((8, columns), f32)
    for k, row in enumerate(rows):
        out = jnp.where(index == k, row, out)
    return [out, jnp.zeros((8, columns), f32)]


def three(values):
    return [part.astype(f32) for part in split3(values)]


def feature_tile(points, omega, phase, total):
    turn = 1.0 / (2.0 * math.pi)
    ones = [1.0] * 3
    left = left_stack(points, eight_rows(ones, points.shape[1]))
    right = right_stack(omega * turn, eight_rows(three(phase * turn), omega.shape[1]))
    turns = lax.dot_general(
        left.astype(f32).T.astype(bf16), right, (((1,), (0,)), ((), ())), preferred_element_type=f32
    )
    rest = turns - jnp.round(turns)
    square = rest * rest
    scale = math.sqrt(2.0 / total)
    value = jnp.full(square.shape, COS[-1] * scale, f32)
    for coefficient in COS[-2::-1]:
        value = value * square + coefficient * scale
    return value.astype(bf16)


def prior_kernel(
    which, x_hbm, omega_hbm, phase_hbm, weights_hbm, targets_hbm, noise_hbm, out_ref,
    x_ref, omega_ref, phase_ref, weights_ref, targets_ref, noise_ref, arrived,
):
    half = weights_hbm.shape[1]
    columns = pl.ds(pl.multiple_of(which[0] * half, 128), half)
    copies = [
        pltpu.make_async_copy(source, target, arrived.at[k])
        for k, (source, target) in enumerate((
            (x_hbm, x_ref),
            (omega_hbm.at[:, columns], omega_ref),
            (phase_hbm.at[:, columns], phase_ref),
            (weights_hbm, weights_ref),
            (targets_hbm, targets_ref),
            (noise_hbm, noise_ref),
        ))
    ]
    for copy in copies:
        copy.start()
    for copy in copies[:3]:
        copy.wait()
    feats = feature_tile(x_ref[...], omega_ref[...], phase_ref[...], omega_hbm.shape[1])
    for copy in copies[3:]:
        copy.wait()
    prior = lax.dot_general(weights_ref[...], feats, (((1,), (1,)), ((), ())), preferred_element_type=f32)
    own = targets_ref[...] - noise_ref[...].T
    repeats = out_ref.shape[1] // own.shape[1]
    lane = lax.broadcasted_iota(jnp.int32, out_ref.shape, 1)
    here = lane // own.shape[1] == which[0]
    out_ref[...] = jnp.where(here, jnp.concatenate([own] * repeats, axis=1), 0.0) - prior


def pack_kernel(mine_ref, other_ref, x_ref, pair_ref, payload_ref):
    samples, dim = mine_ref.shape[0], x_ref.shape[0]
    payload_ref[:samples, :] = mine_ref[...] + other_ref[...]
    payload_ref[samples : samples + dim, :] = x_ref[...]
    payload_ref[samples + dim :, :] = pair_ref[...]


def cand_kernel(which, x_ref, omega_ref, phase_ref, mine_ref, other_ref, out_ref):
    half = mine_ref.shape[1]
    total = omega_ref.shape[1]
    here = pl.multiple_of(which[0] * half, 128)
    there = pl.multiple_of((1 - which[0]) * half, 128)
    out = None
    for start, weights in ((here, mine_ref), (there, other_ref)):
        feats = feature_tile(x_ref[...], omega_ref[:, pl.ds(start, half)], phase_ref[:, pl.ds(start, half)], total)
        part = lax.dot_general(feats, weights[...], (((1,), (1,)), ((), ())), preferred_element_type=f32)
        out = part if out is None else out + part
    out_ref[...] = out


def halves_of(points):
    return three((-0.5 * LOG2E) * jnp.sum(points * points, axis=0, keepdims=True))


def left_of(points):
    stack = left_stack(points * LOG2E, eight_rows(halves_of(points) + [1.0] * 3, points.shape[1]))
    return stack.astype(f32).T.astype(bf16)


def right_of(points):
    return right_stack(points, eight_rows([1.0] * 3 + halves_of(points), points.shape[1]))


def fill(out_ref, left_ref, right_ref, transposed_ref=None):
    rows, columns = out_ref.shape
    for i in range(0, rows, TILE):
        for j in range(i if transposed_ref is out_ref else 0, columns, TILE):
            height, width = min(TILE, rows - i), min(TILE, columns - j)
            exponent = jnp.dot(
                left_ref[i : i + height, :], right_ref[:, j : j + width], preferred_element_type=f32
            )
            tile = jnp.exp2(exponent).astype(bf16)
            out_ref[i : i + height, j : j + width] = tile
            if transposed_ref is not None and (transposed_ref is not out_ref or j > i):
                transposed_ref[j : j + width, i : i + height] = tile.T


def points_of(block_ref, samples):
    dim = (block_ref.shape[1] - samples) // 2
    return jnp.concatenate(
        [block_ref[k, samples : samples + dim, :] for k in range(block_ref.shape[0])]
        + [block_ref[k, samples + dim :, :] for k in range(block_ref.shape[0])],
        axis=1,
    )


def rows_of(block_ref, samples, first=0, last=None):
    last = block_ref.shape[0] if last is None else last
    return jnp.concatenate([block_ref[k, :samples, :] for k in range(first, last)], axis=1)


def product(rows, kernel):
    return jnp.dot(rows, kernel, preferred_element_type=f32)


def product_transposed(rows, kernel):
    return lax.dot_general(rows, kernel, (((1,), (1,)), ((), ())), preferred_element_type=f32)


def near_kernel(
    block_ref, cand_ref, left_ref, right_ref, cand_left_ref, kernel_ref, tile_ref, field_ref
):
    samples = field_ref.shape[0]
    points = points_of(block_ref, samples)
    left_ref[...] = left_of(points)
    right_ref[...] = right_of(points)
    cand_left_ref[...] = left_of(cand_ref[...])
    fill(kernel_ref, left_ref, right_ref)
    fill(tile_ref, cand_left_ref, right_ref)
    half = points.shape[1] // 2
    field_ref[...] = product(rows_of(block_ref, samples).astype(bf16), kernel_ref[:half, :])


def side_kernel(
    block_ref, near_ref, left_ref, right_ref, cand_left_ref,
    side_left_ref, side_right_ref, near_side_ref, side_near_ref, side_ref, tile_ref, field_ref,
):
    samples, size = field_ref.shape
    points = points_of(block_ref, samples)
    side_left_ref[...] = left_of(points)
    side_right_ref[...] = right_of(points)
    fill(near_side_ref, left_ref, side_right_ref, side_near_ref)
    fill(side_ref, side_left_ref, side_right_ref, side_ref)
    fill(tile_ref, cand_left_ref, side_right_ref)
    near, side = rows_of(near_ref, samples).astype(bf16), rows_of(block_ref, samples).astype(bf16)
    field_ref[...] = product(near, near_side_ref[: near.shape[1], :]) + product(side, side_ref[: size // 2, :])


def last_kernel(
    block_ref, near_ref, side_block_ref, left_ref, right_ref, cand_left_ref, side_left_ref, side_right_ref,
    near_before_ref, side_before_ref, near_other_ref, near_near_ref, side_near_ref,
    near_last_ref, last_near_ref, side_last_ref, last_side_ref, last_ref, tile_ref, field_ref,
    last_left_ref, last_right_ref,
):
    samples = field_ref.shape[0]
    points = points_of(block_ref, samples)
    last_left_ref[...] = left_of(points)
    last_right_ref[...] = right_of(points)
    fill(near_last_ref, left_ref, last_right_ref, last_near_ref)
    fill(side_last_ref, side_left_ref, last_right_ref, last_side_ref)
    fill(last_ref, last_left_ref, last_right_ref, last_ref)
    fill(tile_ref, cand_left_ref, last_right_ref)
    count, size = near_before_ref.shape[1], points.shape[1]
    half = size // 2
    near, side, last = (
        rows_of(ref, samples).astype(bf16) for ref in (near_ref, side_block_ref, block_ref)
    )
    other = rows_of(near_other_ref, samples).astype(bf16)
    field_ref[:, :count] = (
        near_before_ref[...]
        + product(side, side_near_ref[:half, :])
        + product(last, last_near_ref[:half, :])
        + product(other, near_near_ref[size:, :])
    )
    field_ref[:, count : count + size] = side_before_ref[...] + product(last, last_side_ref[:half, :])
    field_ref[:, count + size :] = (
        product(near, near_last_ref[: near.shape[1], :])
        + product(side, side_last_ref[:half, :])
        + product(last, last_ref[:half, :])
    )


def solve_kernel(
    own_rows, which, near_ref, side_block_ref, last_block_ref, near_other_ref, far_other_ref, before_ref,
    near_near_ref, near_side_ref, side_near_ref, side_ref,
    near_last_ref, last_near_ref, side_last_ref, last_side_ref, last_ref,
    near_tile_ref, side_tile_ref, last_tile_ref, prior_ref, samples_ref, solution_ref,
    image_ref, start_ref, direction_ref, packed_ref,
):
    samples = prior_ref.shape[1]
    width = near_ref.shape[2]
    count, size = near_side_ref.shape
    half = size // 2
    few = half // width
    position = 0
    for block_ref, first, blocks in (
        (near_ref, 0, 2 * few), (near_other_ref, 0, 2 * few),
        (side_block_ref, 0, few), (far_other_ref, few, few),
        (last_block_ref, 0, few), (far_other_ref, 0, few),
    ):
        for k in range(first, first + blocks):
            start_ref[:, position : position + width] = block_ref[k, :samples, :]
            position += width
    near = start_ref[:, size:count].astype(bf16)
    side = start_ref[:, count + half : count + size].astype(bf16)
    last = start_ref[:, count + size + half :].astype(bf16)
    segments = (
        (0, count, ((side, side_near_ref, half), (last, last_near_ref, half)), (), near_near_ref, near_tile_ref),
        (
            count, size,
            ((near, near_side_ref, size), (side, side_ref, half), (last, last_side_ref, half)),
            ((0, near_side_ref),), side_ref, side_tile_ref,
        ),
        (
            count + size, size,
            ((near, near_last_ref, size), (side, side_last_ref, half), (last, last_ref, half)),
            ((0, near_last_ref), (count, side_last_ref)), last_ref, last_tile_ref,
        ),
    )
    tiles = [
        (slice(offset + j, offset + j + TILE), slice(j, j + TILE), offset, *segment)
        for offset, extent, *segment in segments
        for j in range(0, extent, TILE)
    ]

    def total(values):
        return jnp.sum(values, axis=1, keepdims=True)

    zero = jnp.zeros((samples, TILE), f32)
    norm0, curve0, norm1, curve1 = zero, zero, zero, zero
    for columns, inner, _, products, *_ in tiles:
        value = before_ref[:, columns]
        for rows, kernel_ref, first in products:
            value += product(rows, kernel_ref[first:, inner])
        start = start_ref[:, columns]
        image = value + noise_level * start
        image_ref[:, columns] = image
        norm0 += start * start
        curve0 += start * image
    norm0 = total(norm0)
    alpha0 = norm0 / total(curve0)
    for columns, *_ in tiles:
        residual = start_ref[:, columns] - alpha0 * image_ref[:, columns]
        direction_ref[:, columns] = residual
        norm1 += residual * residual
    norm1 = total(norm1)
    beta = norm1 / norm0
    for columns, *_ in tiles:
        direction = direction_ref[:, columns] + beta * start_ref[:, columns]
        direction_ref[:, columns] = direction
        packed_ref[:, columns] = direction.astype(bf16)

    for columns, inner, offset, _, above, diagonal, _ in tiles:
        value = product(packed_ref[:, columns], diagonal[inner, inner])
        for first, kernel_ref in above:
            rows = packed_ref[:, first : first + kernel_ref.shape[0]]
            value += 2.0 * product(rows, kernel_ref[:, inner])
        if inner.start:
            rows = packed_ref[:, offset : offset + inner.start]
            value += 2.0 * product(rows, diagonal[: inner.start, inner])
        direction = direction_ref[:, columns]
        curve1 += direction * (value + noise_level * direction)
    alpha1 = norm1 / total(curve1)
    own = (alpha0 * start_ref[:, :width] + alpha1 * direction_ref[:, :width]).T
    solution_ref[...] = jnp.where(which[0] == 0, own[:own_rows], own[own_rows:])
    value = prior_ref[...]
    for columns, inner, *_, tile_ref in tiles:
        weights = (alpha0 * start_ref[:, columns] + alpha1 * direction_ref[:, columns]).astype(bf16)
        value += product_transposed(tile_ref[:, inner], weights)
    samples_ref[...] = value


def call(kernel, out_shape, inputs, scratch=(), scalars=0, hbm=False, flops=0):
    vmem = pl.BlockSpec(memory_space=pltpu.VMEM)
    smem = pl.BlockSpec(memory_space=pltpu.SMEM)
    source = pl.BlockSpec(memory_space=pltpu.HBM) if hbm else vmem
    return pl.pallas_call(
        kernel,
        out_shape=out_shape,
        in_specs=[smem] * scalars + [source] * inputs,
        out_specs=jax.tree.map(lambda _: vmem, out_shape),
        scratch_shapes=list(scratch),
        cost_estimate=pl.CostEstimate(flops=flops, transcendentals=0, bytes_accessed=1 << 20),
        compiler_params=pltpu.CompilerParams(vmem_limit_bytes=16 << 20),
    )


def local_body(x_train, x_cand, targets, noise, omega, phase, prior_weights):
    own_rows, samples = noise.shape
    dim, width = x_train.shape
    blocks = lax.axis_size("train")
    cand_index = lax.axis_index("cand")
    train_index = lax.axis_index("train")
    which = cand_index.astype(jnp.int32).reshape(1)
    phase = phase.reshape(1, -1)
    weights = prior_weights.T
    half_features = weights.shape[1]
    shape = jax.ShapeDtypeStruct
    swap = [(0, 1), (1, 0)]

    def in_hbm(values):
        return pltpu.with_memory_space_constraint(values, pltpu.HBM)

    def exchange(values, bit):
        return lax.ppermute(values, "train", [(i, i ^ bit) for i in range(blocks)])

    pair = exchange(x_train, 1)
    partial = call(
        prior_kernel,
        shape((samples, width), f32),
        scalars=1, inputs=6, hbm=True, flops=1 << 30,
        scratch=[
            pltpu.VMEM((dim, width), f32),
            pltpu.VMEM((dim, half_features), f32),
            pltpu.VMEM((1, half_features), f32),
            pltpu.VMEM(weights.shape, bf16),
            pltpu.VMEM((1, own_rows), f32),
            pltpu.VMEM(noise.shape, f32),
            pltpu.SemaphoreType.DMA((6,)),
        ],
    )(which, *map(in_hbm, (x_train, omega, phase, weights, targets.reshape(1, -1), noise)))
    other = lax.ppermute(partial, "cand", swap)
    payload = call(pack_kernel, shape((samples + 2 * dim, width), f32), inputs=4)(
        partial, other, x_train, pair
    )
    other_weights = lax.ppermute(weights, "cand", swap)
    first = payload[None]
    bit = blocks // 2
    while bit > 4:
        moved = exchange(first, bit)
        first = jnp.concatenate([first, moved], axis=0)
        bit //= 2
    third = exchange(first, 6)
    second = exchange(first, 4)
    near = jnp.concatenate([first, exchange(first, 2)], axis=0)
    per_device = x_cand.shape[1] // blocks
    mine = lax.dynamic_slice_in_dim(x_cand, train_index * per_device, per_device, 1)
    prior_cand = call(cand_kernel, shape((per_device, samples), f32), scalars=1, inputs=5, flops=1 << 30)(
        which, mine, omega, phase, weights, other_weights
    )
    count = blocks * width // 2
    stack = 6 * dim + 16
    square = shape((count, count), bf16)
    left, right, cand_left, near_near, near_tile, before = call(
        near_kernel,
        (
            shape((count, stack), bf16),
            shape((stack, count), bf16),
            shape((per_device, stack), bf16),
            square,
            shape((per_device, count), bf16),
            shape((samples, count), f32),
        ),
        inputs=2, flops=1 << 31,
    )(near, mine)
    near_other = exchange(near[:, :samples], 1)
    size = count // 2

    def kernels(*shapes):
        return tuple(shape(dims, bf16) for dims in shapes)

    (side_left, side_right, near_side, side_near, side, side_tile, side_before) = call(
        side_kernel,
        kernels((size, stack), (stack, size), (count, size), (size, count), (size, size), (per_device, size))
        + (shape((samples, size), f32),),
        inputs=5, flops=1 << 31,
    )(third, near, left, right, cand_left)
    far_other = exchange(jnp.concatenate([second[:, :samples], third[:, :samples]], axis=0), 1)
    near_last, last_near, side_last, last_side, last, last_tile, before = call(
        last_kernel,
        kernels((count, size), (size, count), (size, size), (size, size), (size, size), (per_device, size))
        + (shape((samples, 2 * count), f32),),
        scratch=[pltpu.VMEM((size, stack), bf16), pltpu.VMEM((stack, size), bf16)],
        inputs=13, flops=1 << 32,
    )(
        second, near, third, left, right, cand_left, side_left, side_right, before, side_before,
        near_other, near_near, side_near,
    )
    return tuple(
        call(
            functools.partial(solve_kernel, own_rows),
            (shape((per_device, samples), f32), shape((own_rows, samples), f32)),
            scratch=[
                pltpu.VMEM((samples, 2 * count), f32),
                pltpu.VMEM((samples, 2 * count), f32),
                pltpu.VMEM((samples, 2 * count), f32),
                pltpu.VMEM((samples, 2 * count), bf16),
            ],
            scalars=1, inputs=19, flops=1 << 33,
        )(
            which, near, third, second, near_other, far_other, before,
            near_near, near_side, side_near, side,
            near_last, last_near, side_last, last_side, last,
            near_tile, side_tile, last_tile, prior_cand,
        )
    )


def is_local(mesh, x_train):
    train, cand = mesh.shape["train"], mesh.shape["cand"]
    count = x_train.shape[1]
    tiles = count // 4 % TILE == 0
    return cand == 2 and train >= 8 and train & (train - 1) == 0 and tiles and 2 * count * count <= KERNEL_BYTES


def squares_of(points):
    return jnp.sum(points * points, axis=0)


def kernel_tile(row_points, row_norms, column_points, column_norms):
    inner = jnp.dot(row_points.T, column_points, precision=lax.Precision.HIGHEST)
    return jnp.exp(-0.5 * (row_norms[:, None] + column_norms[None, :] - 2.0 * inner)).astype(
        jnp.bfloat16
    )


def features(points, omega, phase):
    angles = jnp.dot(points.T, omega, precision=lax.Precision.HIGHEST) + phase[None, :]
    return (math.sqrt(2.0 / omega.shape[1]) * jnp.cos(angles)).astype(jnp.bfloat16)


def kernel_rows(points, every_point, every_norm, weights):
    count = points.shape[1]
    size = math.gcd(count, 1024)
    stacked = points.reshape(points.shape[0], count // size, size).transpose(1, 0, 2)

    def one_block(block_points):
        tile = kernel_tile(block_points, squares_of(block_points), every_point, every_norm)
        return jnp.dot(tile, weights, preferred_element_type=jnp.float32)

    return lax.map(one_block, stacked).reshape(count, weights.shape[1])


def body(x_train, x_cand, targets, noise, omega, phase, prior_weights):
    own_rows = noise.shape[0]
    cand_index = lax.axis_index("cand")
    train_index = lax.axis_index("train")
    own_points = lax.dynamic_slice_in_dim(x_train, cand_index * own_rows, own_rows, 1)
    full_weights = lax.all_gather(prior_weights, "cand", axis=0, tiled=True)
    prior_train = jnp.dot(
        features(own_points, omega, phase), full_weights, preferred_element_type=jnp.float32
    )
    rhs = targets[:, None] - prior_train - noise
    column_points = lax.all_gather(own_points, "train", axis=1, tiled=True)
    row_norms = squares_of(x_train)
    column_norms = squares_of(column_points)
    width = max(128, 262144 // x_train.shape[1])

    def squares(values):
        return lax.psum(jnp.sum(values * values, axis=0), ("train", "cand"))

    solution = jnp.zeros(rhs.shape, jnp.float32)
    residual = rhs
    direction = rhs
    norm_now = squares(residual)
    for _ in range(ITERS):
        packed = direction.astype(jnp.bfloat16)
        empty = jnp.zeros((x_train.shape[1], packed.shape[1]), jnp.float32)
        total = empty
        piece = lax.all_gather(packed, "train", axis=0, tiled=True)
        for offset in range(0, piece.shape[0], width):
            count = min(width, piece.shape[0] - offset)
            accumulate_points = lax.dynamic_slice_in_dim(column_points, offset, count, 1)
            norms = lax.dynamic_slice_in_dim(column_norms, offset, count, 0)
            tile = kernel_tile(x_train, row_norms, accumulate_points, norms)
            total = total + jnp.dot(
                tile, piece[offset : offset + count], preferred_element_type=jnp.float32
            )
        apply_total = total
        apply_total = lax.psum_scatter(apply_total, "cand", scatter_dimension=0, tiled=True)
        image = apply_total + noise_level * direction
        curve = lax.psum(jnp.sum(direction * image, axis=0), ("train", "cand"))
        alpha = norm_now / curve
        solution = solution + alpha * direction
        residual = residual - alpha * image
        norm_next = squares(residual)
        direction = residual + norm_next / norm_now * direction
        norm_now = norm_next
    per_device = x_cand.shape[1] // lax.axis_size("train")
    mine = lax.dynamic_slice_in_dim(x_cand, train_index * per_device, per_device, 1)
    packed_solution = solution.astype(jnp.bfloat16)
    block_weights = lax.all_gather(packed_solution, "cand", axis=0, tiled=True)
    train_norms = squares_of(x_train)
    kernel_part = lax.psum_scatter(
        kernel_rows(x_cand, x_train, train_norms, block_weights),
        "train",
        scatter_dimension=0,
        tiled=True,
    )
    prior_cand = jnp.dot(
        features(mine, omega, phase), full_weights, preferred_element_type=jnp.float32
    )
    return (prior_cand + kernel_part, solution)


def solution(mesh):
    placed = (
        P(None, "train"),
        P(None, "cand"),
        P(("train", "cand")),
        P(("train", "cand"), None),
        P(),
        P(),
        P("cand", None),
    )

    def sharded(chosen):
        return jax.shard_map(
            chosen,
            mesh=mesh,
            in_specs=placed,
            out_specs=(P(("cand", "train"), None), P(("train", "cand"), None)),
            check_vma=False,
        )

    def step(x_train, *rest):
        if not is_local(mesh, x_train):
            return sharded(body)(x_train, *rest)
        return sharded(local_body)(x_train, *rest)

    return step
```
